32 devices in a mesh: row: 4 (over x, core), col: 8 (over z, y).
Axes of the slice: x: 2, y: 2, z: 4, core: 2. Of those that a mesh axis runs over, the one named last changes fastest.
Arguments:
- object_field: float32 [2, 2048, 4096], P(None, 'row', 'col'), may hold values from -6 to 6
- probe: float32 [2, 256, 256], replicated, may hold values from -6 to 6
- dual: float32 [2, 4, 8, 4, 256, 256], P(None, 'row', 'col'), may hold values from -4 to 4
- amplitude: float32 [4, 8, 4, 256, 256], P('row', 'col'), may hold values from 0.1 to 3
- offsets: int32 [2, 4, 8, 4], P(None, 'row', 'col'), may hold values from 0 to 511
- live: int32 [4, 8], P('row', 'col'), may hold values from 1 to 4, as said below
Outputs:
- object_new: float32 [2, 2048, 4096], P(None, 'row', 'col')
- dual_new: float32 [2, 4, 8, 4, 256, 256], P(None, 'row', 'col')
The draws below stay inside these ranges and needn't reach their ends.
Inputs may be any that keep to these rules, and one draw needn't show every extreme that they name: `offsets`: each slot's probe centre lies inside its own tile. `live`: the used slots of a tile are its first ones; some tile uses all 4 slots.
All inputs are finite; a program needn't handle non-finite values.
Results may differ from the reference program's by a relative error of at most 0.00022.
Values sent between devices are 32-bit elements; how exact they have to be, the bound alone decides.
A program may use at most 128 MiB of HBM per device.

```python
import math
import jax
import jax.numpy as jnp
from jax import lax

PS = 256
TILE = 512
NP = 4
GRID_R = 4
GRID_C = 8
NR = 2048
NC = 4096


def draw_live(key, part):
    first, second = jax.random.split(jax.random.fold_in(key, 7))
    counts = jax.random.randint(first, (GRID_R * GRID_C,), 1, NP + 1)
    chosen = jax.random.randint(second, (), 0, GRID_R * GRID_C)
    counts = jnp.where(jnp.arange(GRID_R * GRID_C) == chosen, NP, counts)
    return counts.reshape(GRID_R, GRID_C).astype(jnp.int32)


def with_ends(result, own_key, least, high):
    shape = result.shape
    spot = [jax.random.randint(jax.random.fold_in(own_key, axis), (), 0, shape[axis]) for axis in range(len(shape))]
    result = result.at[tuple(spot)].set(least)
    longest = shape.index(max(shape))
    spot[longest] = (spot[longest] + 1) % shape[longest]
    return result.at[tuple(spot)].set(high)


def steps_of(rng, shape, cuts, smallest, high):
    loudness, own = 1.0, jax.random.fold_in(rng, 6)
    for axis_at, blocks in cuts:
        heights = jnp.exp(jax.random.uniform(jax.random.fold_in(own, axis_at), (blocks,), jnp.float32, smallest / len(cuts), high / len(cuts)))
        loudness = loudness * jnp.repeat(heights, shape[axis_at] // blocks).reshape([-1 if axis == axis_at else 1 for axis in range(len(shape))])
    return loudness


def bell_draw(key, extent, spread, limit, cuts=(), kind=jnp.bfloat16):
    factor_of = steps_of(key, extent, cuts, -0.22, 0.18) if cuts else 1.0
    drawn = jax.random.normal(key, extent, jnp.float32) * spread * factor_of
    return jnp.minimum(jnp.maximum(drawn, -limit), limit).astype(kind)


def setup_inputs(seed: int = 0) -> dict:
    keys = jax.random.split(jax.random.key(seed), 7)
    return {
        "object_field": bell_draw(keys[0], (2, NR, NC), 1.0, 6.0, ((1, 4), (2, 8)), jnp.float32),
        "probe": bell_draw(keys[1], (2, PS, PS), 1.0, 6.0, (), jnp.float32),
        "dual": bell_draw(keys[2], (2, GRID_R, GRID_C, NP, PS, PS), 0.5, 4.0, ((1, 4), (2, 8)), jnp.float32),
        "amplitude": jnp.clip(jnp.exp(math.log(3.0) - 3.4011974 * jax.random.uniform(keys[3], (GRID_R, GRID_C, NP, PS, PS), jnp.float32) ** steps_of(keys[3], (GRID_R, GRID_C, NP, PS, PS), ((0, 4), (1, 8)), -0.2, 0.2)), 0.1, 3.0),
        "offsets": with_ends(jax.random.randint(keys[4], (2, GRID_R, GRID_C, NP), 0, TILE), jax.random.fold_in(keys[4], 1), 0, TILE - 1).astype(jnp.int32),
        "live": draw_live(jax.random.fold_in(keys[6], 71), 0),
    }


FLOOR = 0.1
BETA = 1.0


def reference(object_field, probe, dual, amplitude, offsets, live):
    half = PS // 2
    count = GRID_R * GRID_C * NP
    probe_c = probe[0] + 1j * probe[1]
    power = probe[0] * probe[0] + probe[1] * probe[1]
    padded = jnp.pad(object_field, ((0, 0), (half, half), (half, half)))
    tops = ((jnp.arange(GRID_R) * TILE)[:, None, None] + offsets[0]).astype(jnp.int32).reshape(count)
    lefts = ((jnp.arange(GRID_C) * TILE)[None, :, None] + offsets[1]).astype(jnp.int32).reshape(count)
    used = (jnp.arange(NP)[None, None, :] < live[:, :, None]).astype(object_field.dtype).reshape(count)
    duals = jnp.moveaxis(dual, 0, 3).reshape(count, 2, PS, PS)
    amps = amplitude.reshape(count, PS, PS)
    zero = jnp.int32(0)

    def forward(acc, item):
        top, left, lam, amp, use = item
        patch = lax.dynamic_slice(padded, (zero, top, left), (2, PS, PS))
        lam_c = lam[0] + 1j * lam[1]
        wave = probe_c * (patch[0] + 1j * patch[1]) + lam_c
        spec = jnp.fft.fft2(wave, norm="ortho")
        spec = amp * spec / jnp.maximum(jnp.abs(spec), FLOOR)
        exit_wave = jnp.fft.ifft2(spec, norm="ortho")
        diff = jnp.conj(probe_c) * (exit_wave - lam_c)
        piece = use * jnp.stack((diff.real, diff.imag, power))
        current = lax.dynamic_slice(acc, (zero, top, left), (3, PS, PS))
        acc = lax.dynamic_update_slice(acc, current + piece, (zero, top, left))
        return acc, jnp.stack((exit_wave.real, exit_wave.imag))

    start = jnp.zeros((3, GRID_R * TILE + PS, GRID_C * TILE + PS), object_field.dtype)
    acc, exits = lax.scan(forward, start, (tops, lefts, duals, amps, used))
    sums = acc[:, half:half + GRID_R * TILE, half:half + GRID_C * TILE]
    object_new = (sums[:2] + BETA * object_field) / (sums[2] + BETA)
    padded_new = jnp.pad(object_new, ((0, 0), (half, half), (half, half)))

    def backward(item):
        top, left, lam, exit_wave, use = item
        patch = lax.dynamic_slice(padded_new, (zero, top, left), (2, PS, PS))
        lit = probe_c * (patch[0] + 1j * patch[1])
        return lam + use * (jnp.stack((lit.real, lit.imag)) - exit_wave)

    dual_new = lax.map(backward, (tops, lefts, duals, exits, used))
    dual_new = jnp.moveaxis(dual_new.reshape(GRID_R, GRID_C, NP, 2, PS, PS), 3, 0)
    return (object_new, dual_new)
```

```python
import functools
import math

import jax
import jax.numpy as jnp
import numpy as np
from jax import lax
from jax.experimental import pallas as pl
from jax.experimental.pallas import tpu as pltpu
from jax.sharding import PartitionSpec as P

FLOOR = 0.1
BETA = 1.0
LANES = 128
ROWS = 8
MIB = 1 << 20
F32 = jnp.float32
BF16 = jnp.bfloat16
ANY = pl.BlockSpec(memory_space=pl.ANY)
VM = pl.BlockSpec(memory_space=pltpu.VMEM)
SM = pl.BlockSpec(memory_space=pltpu.SMEM)
HBM = pl.BlockSpec(memory_space=pltpu.HBM)


def tables(size):
    n = size // 2
    k = np.arange(n)
    angle = 2.0 * math.pi * ((k[:, None] * k[None, :]) % n) / n
    c, s = np.cos(angle) / math.sqrt(size), np.sin(angle) / math.sqrt(size)
    fwd = np.block([[c, s], [-s, c]])
    inv = np.block([[c, -s], [s, c]])
    parts = []
    for full in (fwd, inv):
        hi = full.astype(np.float32).astype(BF16)
        parts += [hi, (full - hi.astype(np.float64)).astype(np.float32).astype(BF16)]
    perm = np.zeros((size, size), np.float32)
    perm[2 * k, k] = 1.0
    perm[2 * k + 1, n + k] = 1.0
    tw = 2.0 * math.pi * k / size
    ct, st = np.cos(tw).astype(np.float32), np.sin(tw).astype(np.float32)
    rows = np.stack([np.broadcast_to(ct[:, None], (n, size)), np.broadcast_to(st[:, None], (n, size))])
    both = np.broadcast_to(np.concatenate([ct, st])[None, :], (n, size))
    waves = np.concatenate([rows, both[None]]).astype(np.float32)
    return [jnp.asarray(np.stack(parts + [perm.astype(BF16)])), jnp.asarray(waves)]


def split(x):
    hi = x.astype(BF16)
    return hi, (x - hi.astype(F32)).astype(BF16)


def dot(a, b):
    return jnp.dot(a, b, preferred_element_type=F32)


def left_dot(wh, wl, x):
    xh, xl = split(x)
    return dot(wl, xh) + dot(wh, xl) + dot(wh, xh)


def right_dot(x, wh, wl):
    xh, xl = split(x)
    return dot(xh, wl) + dot(xl, wh) + dot(xh, wh)


def cat(parts, axis):
    return jnp.concatenate(parts, axis=axis)


def load_window(ext, channel, top, left, size):
    row = pl.multiple_of((top // ROWS) * ROWS, ROWS)
    base = pl.multiple_of((left // LANES) * LANES, LANES)
    width, height = size + LANES, size + ROWS
    wide = ext[channel, pl.ds(row, height), pl.ds(base, width)]
    wide = pltpu.roll(wide, (width - (left - base)) % width, 1)[:, :size]
    return pltpu.roll(wide, (height - (top - row)) % height, 0)[:size]


def add_window(acc, channel, top, left, value):
    size = value.shape[0]
    row = pl.multiple_of((top // ROWS) * ROWS, ROWS)
    base = pl.multiple_of((left // LANES) * LANES, LANES)
    width, height = size + LANES, size + ROWS
    wide = cat([value, jnp.zeros((ROWS, size), F32)], 0)
    wide = pltpu.roll(wide, top - row, 0)
    wide = cat([wide, jnp.zeros((height, LANES), F32)], 1)
    wide = pltpu.roll(wide, left - base, 1)
    acc[channel, pl.ds(row, height), pl.ds(base, width)] += wide


def clear_beyond(grid, tile, half, frame):
    end = half + tile
    strips = (
        ("up", slice(0, half), slice(None)),
        ("down", slice(end, None), slice(None)),
        ("left", slice(half, end), slice(0, half)),
        ("right", slice(half, end), slice(end, None)),
    )
    for side, rows, cols in strips:

        @pl.when(jnp.logical_not(grid.has[side]))
        def _():
            frame[:, rows, cols] = jnp.zeros_like(frame[:, rows, cols])

    for up, rows in (("up", slice(0, half)), ("down", slice(end, None))):
        for side, cols in (("left", slice(0, half)), ("right", slice(end, None))):

            @pl.when(grid.has[up] & jnp.logical_not(grid.has[side]))
            def _():
                frame[:, rows, cols] = jnp.zeros_like(frame[:, rows, cols])


CHUNKS = 4


class Grid:
    def __init__(self, send, recv):
        row, col = lax.axis_index("row"), lax.axis_index("col")
        self.col, self.cols = col, lax.axis_size("col")
        self.has = {
            "up": row > 0,
            "down": row < lax.axis_size("row") - 1,
            "left": col > 0,
            "right": col < self.cols - 1,
        }
        self.peer = {"up": {"row": row - 1}, "down": {"row": row + 1}, "left": {"col": col - 1}, "right": {"col": col + 1}}
        self.back = {"up": "down", "down": "up", "left": "right", "right": "left"}
        self.step = {"left": -1, "right": 1}
        self.send, self.recv = send, recv
        self.count = 0

    def bends(self):
        return self.cols % 2 == 0 and self.cols > 2

    def relayed(self, col, side, rank):
        gaps = self.cols // 2 - 1
        if side == "right":
            share = CHUNKS * (gaps - col // 2) // (gaps + 1)
            return (col % 2 == 1) & (col > 0) & (col < self.cols - 1) & (rank < share)
        share = CHUNKS * (col // 2) // (gaps + 1)
        return (col % 2 == 0) & (col > 0) & (col < self.cols) & (rank < share)

    def greet(self):
        barrier = pltpu.get_barrier_semaphore()
        col = self.col
        signals = [(self.has[side], self.peer[side]) for side in self.has]
        waits = sum(h.astype(jnp.int32) for h in self.has.values())
        if self.bends():
            signals.append((self.relayed(col - 1, "right", 0), {"col": col - 2}))
            signals.append((self.relayed(col + 1, "left", 0), {"col": col + 2}))
            waits += self.relayed(col + 1, "right", 0).astype(jnp.int32)
            waits += self.relayed(col - 1, "left", 0).astype(jnp.int32)
        for goes, peer in signals:

            @pl.when(goes)
            def _():
                pl.semaphore_signal(barrier, inc=1, device_id=peer, device_id_type=pl.DeviceIdType.MESH)

        pl.semaphore_wait(barrier, waits)

    def copy(self, peer, src, dst):
        at = self.count
        self.count += 1
        return pltpu.make_async_remote_copy(
            src_ref=src,
            dst_ref=dst,
            send_sem=self.send.at[at],
            recv_sem=self.recv.at[at],
            device_id=peer,
            device_id_type=pl.DeviceIdType.MESH,
        )

    def message(self, side, src, dst, also=None):
        goes, comes = self.has[side], self.has[self.back[side]]
        if also is not None:
            goes, comes = goes & self.has[also], comes & self.has[also]
        return self.copy(self.peer[side], src, dst), goes, comes

    def strip(self, side, rank, src, dst, relay):
        return Strip(self, side, rank, src, dst, relay)


class Strip:
    def __init__(self, grid, side, rank, src, dst, relay):
        step, col = grid.step[side], grid.col
        goes, comes = grid.has[side], grid.has[grid.back[side]]
        self.hops = []
        if grid.bends() and relay is not None:
            first, then, last = (grid.relayed(col + step * at, side, rank) for at in (0, 1, -1))
            goes, comes = goes & jnp.logical_not(first), comes & jnp.logical_not(last)
            self.hops.append((grid.copy({"col": col - step}, src, relay), first, then))
            self.hops.append((grid.copy({"col": col + 2 * step}, relay, dst), then, last))
        self.direct = grid.copy(grid.peer[side], src, dst), goes, comes

    def start(self):
        start(*self.hops[:1], self.direct)

    def forward(self):
        if self.hops:
            (first, _, comes), (then, _, _) = self.hops

            @pl.when(comes)
            def _():
                first.wait_recv()
                then.start()

    def arrive(self):
        arrive(*self.hops[1:], self.direct)

    def leave(self):
        leave(*self.hops, self.direct)


def when(cond, act):
    if cond is True:
        act()
    else:
        pl.when(cond)(act)


def start(*messages):
    for m in messages:
        if isinstance(m, Strip):
            m.start()
        else:
            pl.when(m[1])(m[0].start)


def forward(*strips):
    for m in strips:
        m.forward()


def arrive(*messages):
    for m in messages:
        if isinstance(m, Strip):
            m.arrive()
        else:
            pl.when(m[2])(m[0].wait_recv)


def leave(*messages):
    for m in messages:
        if isinstance(m, Strip):
            m.leave()
        else:
            pl.when(m[1])(m[0].wait_send)


def column_messages(grid, tile, half, src, frame, relay):
    size, end = 2 * half, half + tile
    mid = (tile - size) // 2
    rows = [slice(half, half + mid), slice(half + mid, tile - half), slice(0, half), slice(tile - half, tile)]
    groups = []
    for rank, at in enumerate(rows):
        store = slice(at.start + half, at.stop + half)
        via = relay[rank] if rank < len(relay) else None
        groups.append(
            [
                grid.strip("left", rank, src.at[:, at, :half], frame.at[:, store, end:], via),
                grid.strip("right", rank, src.at[:, at, tile - half :], frame.at[:, store, :half], via),
            ]
        )
    return groups[2] + groups[3], groups[0] + groups[1]


def row_messages(grid, tile, half, src, frame):
    end = half + tile
    return [
        grid.message("up", src.at[:, :half, :], frame.at[:, end:, half:end]),
        grid.message("down", src.at[:, tile - half :, :], frame.at[:, :half, half:end]),
    ]


def corner_messages(grid, tile, half, frame):
    size, end = 2 * half, half + tile
    out = []
    for side, cols in (("left", slice(0, half)), ("right", slice(end, None))):
        out.append(grid.message("up", frame.at[:, half:size, cols], frame.at[:, end:, cols], also=side))
        out.append(grid.message("down", frame.at[:, tile:end, cols], frame.at[:, :half, cols], also=side))
    return out


def halo_kernel(tile, half, offsets, live, cells, dual, wt, frame, infos, lam, tables_out, tag, r0, r1, r2, send, recv, local):
    grid = Grid(send, recv)
    has = grid.has
    slots = offsets.shape[3]
    loads = [
        pltpu.make_async_copy(cells, frame.at[:, half : half + tile, half : half + tile], local.at[0]),
        pltpu.make_async_copy(dual, lam, local.at[1]),
        pltpu.make_async_copy(wt, tables_out, local.at[2]),
    ]
    lane = lax.broadcasted_iota(jnp.int32, tag.shape, 1)
    value = jnp.where(lane == 2 * slots, live[0, 0], 0)
    for k in range(slots):
        value = jnp.where(lane == k, offsets[0, 0, 0, k], value)
        value = jnp.where(lane == slots + k, offsets[1, 0, 0, k], value)
    tag[...] = value
    infos[1, 1] = value
    ends, inner = column_messages(grid, tile, half, cells, frame, (r0, r1, r2))
    rows = row_messages(grid, tile, half, cells, frame)
    corners = corner_messages(grid, tile, half, frame)
    tags = [
        grid.message("left", tag, infos.at[1, 2]),
        grid.message("right", tag, infos.at[1, 0]),
    ]
    bands = [
        grid.message("up", infos.at[1], infos.at[2]),
        grid.message("down", infos.at[1], infos.at[0]),
    ]
    grid.greet()
    start(*tags, *inner, *ends, *rows)
    for copy in loads:
        copy.start()
    clear_beyond(grid, tile, half, frame)
    for side, at in (("left", (1, 0)), ("right", (1, 2)), ("up", (0,)), ("down", (2,))):

        @pl.when(jnp.logical_not(has[side]))
        def _():
            infos[at] = jnp.zeros_like(infos[at])

    arrive(*tags)
    start(*bands)
    forward(*inner, *ends)
    arrive(*ends)
    start(*corners)
    arrive(*inner, *rows, *bands, *corners)
    for copy in loads:
        copy.wait()
    leave(*tags, *ends, *inner, *rows, *bands, *corners)


def update_kernel(tile, half, *refs):
    acc, cells, weight, frame = refs[:4]
    fa, fb, g_lm, g_rm, g_le, g_re, s_le, s_re, sums, news, send, recv = refs[4:]
    size, end = 2 * half, half + tile
    grid = Grid(send, recv)
    has = grid.has
    val = frame.at[:, half:end, half:end]
    up = grid.message("up", acc.at[:, :half, :], fb)
    down = grid.message("down", acc.at[:, end:, :], fa)
    mid = (tile - size) // 2
    mids = []
    for rank in range(2):
        at, to = slice(size + rank * mid, size + (rank + 1) * mid), slice(rank * mid, (rank + 1) * mid)
        mids.append(grid.strip("left", rank, acc.at[:, at, :half], g_rm.at[:, to], sums.at[rank, :, :mid]))
        mids.append(grid.strip("right", rank, acc.at[:, at, end:], g_lm.at[:, to], sums.at[rank, :, :mid]))
    ends = []
    for at in range(2):
        via = sums.at[2] if at == 0 else None
        ends.append(grid.strip("left", 2 + at, s_le.at[:, at], g_re.at[:, at], via))
        ends.append(grid.strip("right", 2 + at, s_re.at[:, at], g_le.at[:, at], via))
    via = [news.at[0, :, :mid], news.at[1, :, :mid], news.at[2]]
    new_ends, new_inner = column_messages(grid, tile, half, val, frame, via)
    new_rows = row_messages(grid, tile, half, val, frame)
    corners = corner_messages(grid, tile, half, frame)
    grid.greet()
    start(up, down, *mids)
    clear_beyond(grid, tile, half, frame)
    for side, buffers in (("up", (fa,)), ("down", (fb,)), ("left", (g_lm, g_le)), ("right", (g_rm, g_re))):

        @pl.when(jnp.logical_not(has[side]))
        def _():
            for b in buffers:
                b[...] = jnp.zeros_like(b)

    arrive(up, down)
    for ch in range(2):
        s_le[ch, 0] = acc[ch, half:size, :half] + fa[ch, :, :half]
        s_le[ch, 1] = acc[ch, tile:end, :half] + fb[ch, :, :half]
        s_re[ch, 0] = acc[ch, half:size, end:] + fa[ch, :, end:]
        s_re[ch, 1] = acc[ch, tile:end, end:] + fb[ch, :, end:]
    start(*ends)
    tops, bottoms, inner = slice(0, half), slice(tile - half, tile), slice(half, tile - half)
    heads, tails = slice(0, half), slice(tile - half, tile)

    def moved(at):
        return slice(at.start + half, at.stop + half)

    def settle(ch, rows, cols, more):
        total = acc[ch, moved(rows), moved(cols)] + BETA * cells[ch, rows, cols]
        for m in more:
            total = total + m
        frame[ch, moved(rows), moved(cols)] = total / weight[rows, cols]

    forward(*mids)
    for ch in range(2):
        settle(ch, inner, inner, ())
        settle(ch, tops, inner, (fa[ch, :, size:tile],))
        settle(ch, bottoms, inner, (fb[ch, :, size:tile],))
    arrive(*mids)
    for ch in range(2):
        settle(ch, inner, heads, (g_lm[ch],))
        settle(ch, inner, tails, (g_rm[ch],))
    start(*new_inner)
    forward(*ends)
    arrive(*ends)
    for ch in range(2):
        settle(ch, tops, heads, (fa[ch, :, half:size], g_le[ch, 0]))
        settle(ch, bottoms, heads, (fb[ch, :, half:size], g_le[ch, 1]))
        settle(ch, tops, tails, (fa[ch, :, tile:end], g_re[ch, 0]))
        settle(ch, bottoms, tails, (fb[ch, :, tile:end], g_re[ch, 1]))
    start(*new_ends, *new_rows)
    forward(*new_inner, *new_ends)
    arrive(*new_ends)
    start(*corners)
    arrive(*new_inner, *new_rows, *corners)
    leave(up, down, *mids, *ends, *new_ends, *new_inner, *new_rows, *corners)


def add_weights(tile, half, slots, info, acc, power):
    size = 2 * half

    def body(index, carry):
        owner = index // slots
        slot = index % slots
        r, c = owner // 3, owner % 3
        top = info[r, c, 0, slot] + (r - 1) * tile + half
        left = info[r, c, 0, slots + slot] + (c - 1) * tile + half
        live = info[r, c, 0, 2 * slots]
        hit = (slot < live) & (top > 0) & (top < size + tile) & (left > 0) & (left < size + tile)

        @pl.when(hit)
        def _():
            add_window(acc, 0, top, left, power[...])

        return carry

    lax.fori_loop(0, 9 * slots, body, 0)


def project_kernel(tile, half, info, *refs):
    dual, ext, probe, amp, wt, tw = refs[:6]
    base, acc, weight, heavy, power, strips = refs[6:]
    slots = dual.shape[1]
    size = 2 * half
    acc[...] = jnp.zeros_like(acc)
    heavy[...] = jnp.full_like(heavy, BETA)
    power[...] = probe[0] * probe[0] + probe[1] * probe[1]
    add_weights(tile, half, slots, info, heavy, power)
    weight[...] = heavy[0, size : size + tile, size : size + tile]
    live = info[1, 1, 0, 2 * slots]

    def skip(slot, carry):
        base[:, slot] = dual[:, slot]
        return carry

    def many(slots_at):
        tops = [info[1, 1, 0, at] for at in slots_at]
        lefts = [info[1, 1, 0, slots + at] for at in slots_at]
        fh, fl, ih, il = wt[0], wt[1], wt[2], wt[3]
        cr, sr = tw[0], tw[1]
        cc = jnp.broadcast_to(tw[2, :1, :half], (size, half))
        sc = jnp.broadcast_to(tw[2, :1, half:], (size, half))
        n = range(len(slots_at))
        x = []
        for at, top, left in zip(slots_at, tops, lefts):
            pr, pi = probe[0], probe[1]
            wr = load_window(ext, 0, top, left, size)
            wi = load_window(ext, 1, top, left, size)
            re = pr * wr - pi * wi + dual[0, at]
            im = pr * wi + pi * wr + dual[1, at]
            dr, di = re[:half] - re[half:], im[:half] - im[half:]
            x.append(
                cat(
                    [
                        cat([re[:half] + re[half:], dr * cr + di * sr], 1),
                        cat([im[:half] + im[half:], di * cr - dr * sr], 1),
                    ],
                    0,
                )
            )
        y = left_dot(fh, fl, cat(x, 1))
        y = [y[:, 2 * size * i : 2 * size * (i + 1)] for i in n]
        x = []
        for v in y:
            re = cat([v[:half, :size], v[:half, size:]], 0)
            im = cat([v[half:, :size], v[half:, size:]], 0)
            dr, di = re[:, :half] - re[:, half:], im[:, :half] - im[:, half:]
            x.append(cat([re[:, :half] + re[:, half:], im[:, :half] + im[:, half:]], 1))
            x.append(cat([dr * cc + di * sc, di * cc - dr * sc], 1))
        s = right_dot(cat(x, 0), ih, il)
        s = [s[2 * size * i : 2 * size * (i + 1)] for i in n]
        rows = []
        for i, at in enumerate(slots_at):
            for c in range(size // LANES):
                strips[i, c] = amp[at, :, c * LANES : (c + 1) * LANES]
            for first in range(2):
                rows.append(cat([strips[i, c, pl.ds(first, half, stride=2), :] for c in range(size // LANES)], 1))
        ah, al = split(cat(rows, 0))
        a = dot(ah, wt[4]) + dot(al, wt[4])
        x = []
        for i in n:
            b = a[size * i : size * (i + 1)]
            b = cat([b[:, :half], b[:, half:]], 0)
            re, im = s[i][:, :half], s[i][:, half:]
            fac = b * lax.rsqrt(jnp.maximum(re * re + im * im, FLOOR * FLOOR))
            x.append(cat([re * fac, im * fac], 1))
        z = right_dot(cat(x, 0), fh, fl)
        x = []
        for i in n:
            v = z[2 * size * i : 2 * size * (i + 1)]
            er, ei = v[:size, :half], v[:size, half:]
            our, oui = v[size:, :half], v[size:, half:]
            tr, ti = our * cc - oui * sc, oui * cc + our * sc
            re = cat([er + tr, er - tr], 1)
            im = cat([ei + ti, ei - ti], 1)
            x.append(cat([cat([re[:half], re[half:]], 1), cat([im[:half], im[half:]], 1)], 0))
        y = left_dot(ih, il, cat(x, 1))
        for i, (at, top, left) in enumerate(zip(slots_at, tops, lefts)):
            v = y[:, 2 * size * i : 2 * size * (i + 1)]
            er, ei = v[:half, :size], v[half:, :size]
            our, oui = v[:half, size:], v[half:, size:]
            tr, ti = our * cr - oui * sr, oui * cr + our * sr
            dr = cat([er + tr, er - tr], 0) - dual[0, at]
            di = cat([ei + ti, ei - ti], 0) - dual[1, at]
            base[0, at] = -dr
            base[1, at] = -di
            pr, pi = probe[0], probe[1]
            add_window(acc, 0, top, left, pr * dr + pi * di)
            add_window(acc, 1, top, left, pr * di - pi * dr)

    def pair(index, carry):
        many([2 * index, 2 * index + 1])
        return carry

    lax.fori_loop(live, slots, skip, 0)
    lax.fori_loop(0, live // 2, pair, 0)

    @pl.when(live % 2 == 1)
    def _():
        many([live - 1])


def dual_kernel(tile, half, info, ext, probe, base, out, new, ready, sems):
    slots = base.shape[1]
    size = 2 * half
    keep = pltpu.make_async_copy(ext.at[:, half : half + tile, half : half + tile], new, sems.at[slots])
    keep.start()
    copies = []
    for slot in range(slots):
        copy = pltpu.make_async_copy(ready.at[slot], out.at[:, slot], sems.at[slot])
        copies.append(copy)
        active = slot < info[1, 1, 0, 2 * slots]

        @pl.when(jnp.logical_not(active))
        def _():
            ready[slot] = base[:, slot]

        @pl.when(active)
        def _():
            top = info[1, 1, 0, slot]
            left = info[1, 1, 0, slots + slot]
            pr, pi = probe[0], probe[1]
            sr = load_window(ext, 0, top, left, size)
            si = load_window(ext, 1, top, left, size)
            ready[slot, 0] = base[0, slot] + (pr * sr - pi * si)
            ready[slot, 1] = base[1, slot] + (pr * si + pi * sr)

        copy.start()
    for copy in copies:
        copy.wait()
    keep.wait()


def shards(object_field, probe, dual, amplitude, offsets, live):
    tile = object_field.shape[1]
    size = probe.shape[1]
    half = size // 2
    slots = dual.shape[3]
    wide = tile + size
    mid = tile - size
    amps = amplitude.reshape(slots, size, size)
    sd = lambda *shape: jax.ShapeDtypeStruct(shape, F32)
    dma = lambda n: pltpu.SemaphoreType.DMA((n,))
    wt, tw = tables(size)
    fixed = lambda x: pltpu.with_memory_space_constraint(x, pltpu.HBM)

    frame, infos, lam, wt = pl.pallas_call(
        functools.partial(halo_kernel, tile, half),
        out_shape=(
            sd(2, wide, wide),
            jax.ShapeDtypeStruct((3, 3, ROWS, LANES), jnp.int32),
            sd(2, slots, size, size),
            jax.ShapeDtypeStruct(wt.shape, wt.dtype),
        ),
        in_specs=[SM, SM, HBM, HBM, HBM],
        out_specs=(VM, VM, VM, VM),
        scratch_shapes=[
            pltpu.VMEM((ROWS, LANES), jnp.int32),
            pltpu.VMEM((2, mid // 2, half), F32),
            pltpu.VMEM((2, mid // 2, half), F32),
            pltpu.VMEM((2, half, half), F32),
            dma(40),
            dma(40),
            dma(3),
        ],
        compiler_params=pltpu.CompilerParams(collective_id=0, has_side_effects=True, vmem_limit_bytes=16 * MIB),
        cost_estimate=pl.CostEstimate(flops=0, bytes_accessed=80_000_000, transcendentals=0),
        name="halo",
    )(offsets, live, fixed(object_field), fixed(dual.reshape(2, slots, size, size)), fixed(wt))

    cost = lambda size: pl.CostEstimate(flops=0, bytes_accessed=size, transcendentals=0)
    base, acc, weight = pl.pallas_call(
        functools.partial(project_kernel, tile, half),
        out_shape=(sd(2, slots, size, size), sd(2, wide, wide), sd(tile, tile)),
        in_specs=[SM] + [VM] * 6,
        out_specs=(VM, VM, VM),
        scratch_shapes=[
            pltpu.VMEM((1, tile + 2 * size, tile + 2 * size), F32),
            pltpu.VMEM((size, size), F32),
            pltpu.VMEM((2, size // LANES, size, LANES), F32),
        ],
        compiler_params=pltpu.CompilerParams(vmem_limit_bytes=20 * MIB),
        cost_estimate=cost(30_000_000),
        name="project",
    )(infos, lam, frame, probe, amps, wt, tw)

    strip, side, end, via = (2, half, wide), (2, mid, half), (2, 2, half, half), (3, 2, max(half, mid // 2), half)
    frame = pl.pallas_call(
        functools.partial(update_kernel, tile, half),
        out_shape=sd(2, wide, wide),
        in_specs=[VM] * 3,
        out_specs=VM,
        scratch_shapes=[pltpu.VMEM(x, F32) for x in (strip, strip, side, side, end, end, end, end, via, via)] + [dma(60), dma(60)],
        compiler_params=pltpu.CompilerParams(collective_id=1, has_side_effects=True, vmem_limit_bytes=8 * MIB),
        cost_estimate=cost(150_000_000),
        name="update",
    )(acc, object_field, weight)

    dual_new, new = pl.pallas_call(
        functools.partial(dual_kernel, tile, half),
        out_shape=(sd(2, slots, size, size), sd(2, tile, tile)),
        in_specs=[SM, VM, VM, VM],
        out_specs=(ANY, ANY),
        scratch_shapes=[pltpu.VMEM((slots, 2, size, size), F32), dma(slots + 1)],
        compiler_params=pltpu.CompilerParams(vmem_limit_bytes=12 * MIB),
        name="renew",
    )(infos, frame, probe, base)
    return new, dual_new.reshape(dual.shape)


def solution(mesh):
    placed = (
        P(None, "row", "col"),
        P(),
        P(None, "row", "col", None, None, None),
        P("row", "col", None, None, None),
        P(None, "row", "col", None),
        P("row", "col"),
    )
    return jax.shard_map(
        shards,
        mesh=mesh,
        in_specs=placed,
        out_specs=(P(None, "row", "col"), P(None, "row", "col", None, None, None)),
        check_vma=False,
    )
```

```python
import functools
import math

import jax
import jax.numpy as jnp
import numpy as np
from jax import lax
from jax.experimental import pallas as pl
from jax.experimental.pallas import tpu as pltpu
from jax.sharding import PartitionSpec as P

FLOOR = 0.1
BETA = 1.0
LANES = 128
ROWS = 8
MIB = 1 << 20
F32 = jnp.float32
BF16 = jnp.bfloat16
ANY = pl.BlockSpec(memory_space=pl.ANY)
VM = pl.BlockSpec(memory_space=pltpu.VMEM)
SM = pl.BlockSpec(memory_space=pltpu.SMEM)
HBM = pl.BlockSpec(memory_space=pltpu.HBM)


def tables(size):
    n = size // 2
    k = np.arange(n)
    angle = 2.0 * math.pi * ((k[:, None] * k[None, :]) % n) / n
    c, s = np.cos(angle) / math.sqrt(size), np.sin(angle) / math.sqrt(size)
    fwd = np.block([[c, s], [-s, c]])
    inv = np.block([[c, -s], [s, c]])
    parts = []
    for full in (fwd, inv):
        hi = full.astype(np.float32).astype(BF16)
        parts += [hi, (full - hi.astype(np.float64)).astype(np.float32).astype(BF16)]
    perm = np.zeros((size, size), np.float32)
    perm[2 * k, k] = 1.0
    perm[2 * k + 1, n + k] = 1.0
    tw = 2.0 * math.pi * k / size
    ct, st = np.cos(tw).astype(np.float32), np.sin(tw).astype(np.float32)
    rows = np.stack([np.broadcast_to(ct[:, None], (n, size)), np.broadcast_to(st[:, None], (n, size))])
    both = np.broadcast_to(np.concatenate([ct, st])[None, :], (n, size))
    waves = np.concatenate([rows, both[None]]).astype(np.float32)
    return [jnp.asarray(np.stack(parts + [perm.astype(BF16)])), jnp.asarray(waves)]


def split(x):
    hi = x.astype(BF16)
    return hi, (x - hi.astype(F32)).astype(BF16)


def dot(a, b):
    return jnp.dot(a, b, preferred_element_type=F32)


def left_dot(wh, wl, x):
    xh, xl = split(x)
    return dot(wl, xh) + dot(wh, xl) + dot(wh, xh)


def right_dot(x, wh, wl):
    xh, xl = split(x)
    return dot(xh, wl) + dot(xl, wh) + dot(xh, wh)


def cat(parts, axis):
    return jnp.concatenate(parts, axis=axis)


def load_window(ext, channel, top, left, size):
    row = pl.multiple_of((top // ROWS) * ROWS, ROWS)
    base = pl.multiple_of((left // LANES) * LANES, LANES)
    width, height = size + LANES, size + ROWS
    wide = ext[channel, pl.ds(row, height), pl.ds(base, width)]
    wide = pltpu.roll(wide, (width - (left - base)) % width, 1)[:, :size]
    return pltpu.roll(wide, (height - (top - row)) % height, 0)[:size]


def add_window(acc, channel, top, left, value):
    size = value.shape[0]
    row = pl.multiple_of((top // ROWS) * ROWS, ROWS)
    base = pl.multiple_of((left // LANES) * LANES, LANES)
    width, height = size + LANES, size + ROWS
    wide = cat([value, jnp.zeros((ROWS, size), F32)], 0)
    wide = pltpu.roll(wide, top - row, 0)
    wide = cat([wide, jnp.zeros((height, LANES), F32)], 1)
    wide = pltpu.roll(wide, left - base, 1)
    acc[channel, pl.ds(row, height), pl.ds(base, width)] += wide


def clear_beyond(grid, tile, half, frame):
    end = half + tile
    strips = (
        ("up", slice(0, half), slice(None)),
        ("down", slice(end, None), slice(None)),
        ("left", slice(half, end), slice(0, half)),
        ("right", slice(half, end), slice(end, None)),
    )
    for side, rows, cols in strips:

        @pl.when(jnp.logical_not(grid.has[side]))
        def _():
            frame[:, rows, cols] = jnp.zeros_like(frame[:, rows, cols])

    for up, rows in (("up", slice(0, half)), ("down", slice(end, None))):
        for side, cols in (("left", slice(0, half)), ("right", slice(end, None))):

            @pl.when(grid.has[up] & jnp.logical_not(grid.has[side]))
            def _():
                frame[:, rows, cols] = jnp.zeros_like(frame[:, rows, cols])


CHUNKS = 4


class Grid:
    def __init__(self, send, recv):
        row, col = lax.axis_index("row"), lax.axis_index("col")
        self.col, self.cols = col, lax.axis_size("col")
        self.has = {
            "up": row > 0,
            "down": row < lax.axis_size("row") - 1,
            "left": col > 0,
            "right": col < self.cols - 1,
        }
        self.peer = {"up": {"row": row - 1}, "down": {"row": row + 1}, "left": {"col": col - 1}, "right": {"col": col + 1}}
        self.back = {"up": "down", "down": "up", "left": "right", "right": "left"}
        self.step = {"left": -1, "right": 1}
        self.send, self.recv = send, recv
        self.count = 0

    def bends(self):
        return self.cols % 2 == 0 and self.cols > 2

    def relayed(self, col, side, rank):
        gaps = self.cols // 2 - 1
        if side == "right":
            share = CHUNKS * (gaps - col // 2) // (gaps + 1)
            return (col % 2 == 1) & (col > 0) & (col < self.cols - 1) & (rank < share)
        share = CHUNKS * (col // 2) // (gaps + 1)
        return (col % 2 == 0) & (col > 0) & (col < self.cols) & (rank < share)

    def greet(self):
        barrier = pltpu.get_barrier_semaphore()
        col = self.col
        signals = [(self.has[side], self.peer[side]) for side in self.has]
        waits = sum(h.astype(jnp.int32) for h in self.has.values())
        if self.bends():
            signals.append((self.relayed(col - 1, "right", 0), {"col": col - 2}))
            signals.append((self.relayed(col + 1, "left", 0), {"col": col + 2}))
            waits += self.relayed(col + 1, "right", 0).astype(jnp.int32)
            waits += self.relayed(col - 1, "left", 0).astype(jnp.int32)
        for goes, peer in signals:

            @pl.when(goes)
            def _():
                pl.semaphore_signal(barrier, inc=1, device_id=peer, device_id_type=pl.DeviceIdType.MESH)

        pl.semaphore_wait(barrier, waits)

    def copy(self, peer, src, dst):
        at = self.count
        self.count += 1
        return pltpu.make_async_remote_copy(
            src_ref=src,
            dst_ref=dst,
            send_sem=self.send.at[at],
            recv_sem=self.recv.at[at],
            device_id=peer,
            device_id_type=pl.DeviceIdType.MESH,
        )

    def message(self, side, src, dst, also=None):
        goes, comes = self.has[side], self.has[self.back[side]]
        if also is not None:
            goes, comes = goes & self.has[also], comes & self.has[also]
        return self.copy(self.peer[side], src, dst), goes, comes

    def strip(self, side, rank, src, dst, relay):
        return Strip(self, side, rank, src, dst, relay)


class Strip:
    def __init__(self, grid, side, rank, src, dst, relay):
        step, col = grid.step[side], grid.col
        goes, comes = grid.has[side], grid.has[grid.back[side]]
        self.hops = []
        if grid.bends() and relay is not None:
            first, then, last = (grid.relayed(col + step * at, side, rank) for at in (0, 1, -1))
            goes, comes = goes & jnp.logical_not(first), comes & jnp.logical_not(last)
            self.hops.append((grid.copy({"col": col - step}, src, relay), first, then))
            self.hops.append((grid.copy({"col": col + 2 * step}, relay, dst), then, last))
        self.direct = grid.copy(grid.peer[side], src, dst), goes, comes

    def begin(self):
        start(*self.hops[:1])

    def begun(self):
        leave(*self.hops[:1])

    def rest(self):
        start(self.direct)

    def start(self):
        self.begin()
        self.rest()

    def forward(self):
        if self.hops:
            (first, _, comes), (then, _, _) = self.hops

            @pl.when(comes)
            def _():
                first.wait_recv()
                then.start()

    def arrive(self):
        arrive(*self.hops[1:], self.direct)

    def leave(self):
        leave(*self.hops[1:], self.direct)


def when(cond, act):
    if cond is True:
        act()
    else:
        pl.when(cond)(act)


def start(*messages):
    for m in messages:
        if isinstance(m, Strip):
            m.start()
        else:
            pl.when(m[1])(m[0].start)


def each(act, *strips):
    for m in strips:
        getattr(m, act)()


def forward(*strips):
    each("forward", *strips)


def arrive(*messages):
    for m in messages:
        if isinstance(m, Strip):
            m.arrive()
        else:
            pl.when(m[2])(m[0].wait_recv)


def leave(*messages):
    for m in messages:
        if isinstance(m, Strip):
            m.leave()
        else:
            pl.when(m[1])(m[0].wait_send)


def column_messages(grid, tile, half, src, frame, relay):
    size, end = 2 * half, half + tile
    mid = (tile - size) // 2
    rows = [slice(half, half + mid), slice(half + mid, tile - half), slice(0, half), slice(tile - half, tile)]
    groups = []
    for rank, at in enumerate(rows):
        store = slice(at.start + half, at.stop + half)
        via = relay[rank] if rank < len(relay) else None
        groups.append(
            [
                grid.strip("left", rank, src.at[:, at, :half], frame.at[:, store, end:], via),
                grid.strip("right", rank, src.at[:, at, tile - half :], frame.at[:, store, :half], via),
            ]
        )
    return groups[2] + groups[3], groups[0] + groups[1]


def row_messages(grid, tile, half, src, frame):
    end = half + tile
    return [
        grid.message("up", src.at[:, :half, :], frame.at[:, end:, half:end]),
        grid.message("down", src.at[:, tile - half :, :], frame.at[:, :half, half:end]),
    ]


def corner_messages(grid, tile, half, frame):
    size, end = 2 * half, half + tile
    out = []
    for side, cols in (("left", slice(0, half)), ("right", slice(end, None))):
        out.append(grid.message("up", frame.at[:, half:size, cols], frame.at[:, end:, cols], also=side))
        out.append(grid.message("down", frame.at[:, tile:end, cols], frame.at[:, :half, cols], also=side))
    return out


def halo_kernel(tile, half, offsets, live, cells, dual, wt, frame, infos, lam, tables_out, tag, r0, r1, r2, send, recv, local):
    grid = Grid(send, recv)
    has = grid.has
    slots = offsets.shape[3]
    loads = [
        pltpu.make_async_copy(cells, frame.at[:, half : half + tile, half : half + tile], local.at[0]),
        pltpu.make_async_copy(dual, lam, local.at[1]),
        pltpu.make_async_copy(wt, tables_out, local.at[2]),
    ]
    lane = lax.broadcasted_iota(jnp.int32, tag.shape, 1)
    value = jnp.where(lane == 2 * slots, live[0, 0], 0)
    for k in range(slots):
        value = jnp.where(lane == k, offsets[0, 0, 0, k], value)
        value = jnp.where(lane == slots + k, offsets[1, 0, 0, k], value)
    tag[...] = value
    infos[1, 1] = value
    ends, inner = column_messages(grid, tile, half, cells, frame, (r0, r1, r2))
    rows = row_messages(grid, tile, half, cells, frame)
    corners = corner_messages(grid, tile, half, frame)
    tags = [
        grid.message("left", tag, infos.at[1, 2]),
        grid.message("right", tag, infos.at[1, 0]),
    ]
    bands = [
        grid.message("up", infos.at[1], infos.at[2]),
        grid.message("down", infos.at[1], infos.at[0]),
    ]
    grid.greet()
    start(*tags)
    each("begin", *inner, *ends)
    each("rest", *ends)
    start(*rows)
    for copy in loads:
        copy.start()
    clear_beyond(grid, tile, half, frame)
    for side, at in (("left", (1, 0)), ("right", (1, 2)), ("up", (0,)), ("down", (2,))):

        @pl.when(jnp.logical_not(has[side]))
        def _():
            infos[at] = jnp.zeros_like(infos[at])

    arrive(*tags)
    start(*bands)
    each("begun", *inner, *ends)
    each("rest", *inner)
    forward(*inner, *ends)
    arrive(*ends)
    start(*corners)
    arrive(*inner, *rows, *bands, *corners)
    for copy in loads:
        copy.wait()
    leave(*tags, *ends, *inner, *rows, *bands, *corners)


def update_kernel(tile, half, *refs):
    acc, cells, weight, frame = refs[:4]
    fa, fb, g_lm, g_rm, g_le, g_re, s_le, s_re, sums, news, send, recv = refs[4:]
    size, end = 2 * half, half + tile
    grid = Grid(send, recv)
    has = grid.has
    val = frame.at[:, half:end, half:end]
    up = grid.message("up", acc.at[:, :half, :], fb)
    down = grid.message("down", acc.at[:, end:, :], fa)
    mid = (tile - size) // 2
    mids = []
    for rank in range(2):
        at, to = slice(size + rank * mid, size + (rank + 1) * mid), slice(rank * mid, (rank + 1) * mid)
        mids.append(grid.strip("left", rank, acc.at[:, at, :half], g_rm.at[:, to], sums.at[rank, :, :mid]))
        mids.append(grid.strip("right", rank, acc.at[:, at, end:], g_lm.at[:, to], sums.at[rank, :, :mid]))
    ends = []
    for at in range(2):
        via = sums.at[2] if at == 0 else None
        ends.append(grid.strip("left", 2 + at, s_le.at[:, at], g_re.at[:, at], via))
        ends.append(grid.strip("right", 2 + at, s_re.at[:, at], g_le.at[:, at], via))
    via = [news.at[0, :, :mid], news.at[1, :, :mid], news.at[2]]
    new_ends, new_inner = column_messages(grid, tile, half, val, frame, via)
    new_rows = row_messages(grid, tile, half, val, frame)
    corners = corner_messages(grid, tile, half, frame)
    grid.greet()
    each("begin", *mids)
    start(up, down)
    each("rest", *mids)
    clear_beyond(grid, tile, half, frame)
    for side, buffers in (("up", (fa,)), ("down", (fb,)), ("left", (g_lm, g_le)), ("right", (g_rm, g_re))):

        @pl.when(jnp.logical_not(has[side]))
        def _():
            for b in buffers:
                b[...] = jnp.zeros_like(b)

    arrive(up, down)
    for ch in range(2):
        s_le[ch, 0] = acc[ch, half:size, :half] + fa[ch, :, :half]
        s_le[ch, 1] = acc[ch, tile:end, :half] + fb[ch, :, :half]
        s_re[ch, 0] = acc[ch, half:size, end:] + fa[ch, :, end:]
        s_re[ch, 1] = acc[ch, tile:end, end:] + fb[ch, :, end:]
    start(*ends)
    tops, bottoms, inner = slice(0, half), slice(tile - half, tile), slice(half, tile - half)
    heads, tails = slice(0, half), slice(tile - half, tile)

    def moved(at):
        return slice(at.start + half, at.stop + half)

    def settle(ch, rows, cols, more):
        total = acc[ch, moved(rows), moved(cols)] + BETA * cells[ch, rows, cols]
        for m in more:
            total = total + m
        frame[ch, moved(rows), moved(cols)] = total / weight[rows, cols]

    forward(*mids)
    for ch in range(2):
        settle(ch, inner, inner, ())
        settle(ch, tops, inner, (fa[ch, :, size:tile],))
        settle(ch, bottoms, inner, (fb[ch, :, size:tile],))
    arrive(*mids)
    for ch in range(2):
        settle(ch, inner, heads, (g_lm[ch],))
        settle(ch, inner, tails, (g_rm[ch],))
    first, second = [], new_inner
    forward(*ends)
    arrive(*ends)
    for ch in range(2):
        settle(ch, tops, heads, (fa[ch, :, half:size], g_le[ch, 0]))
        settle(ch, bottoms, heads, (fb[ch, :, half:size], g_le[ch, 1]))
        settle(ch, tops, tails, (fa[ch, :, tile:end], g_re[ch, 0]))
        settle(ch, bottoms, tails, (fb[ch, :, tile:end], g_re[ch, 1]))
    each("begin", *new_ends, *second)
    each("rest", *new_ends)
    start(*new_rows)
    forward(*first)
    each("begun", *new_ends, *second)
    each("rest", *second)
    forward(*new_ends, *second)
    arrive(*new_ends)
    start(*corners)
    arrive(*new_inner, *new_rows, *corners)
    each("begun", *mids, *ends, *first)
    leave(up, down, *mids, *ends, *new_ends, *new_inner, *new_rows, *corners)


def add_weights(tile, half, slots, info, acc, power):
    size = 2 * half

    def body(index, carry):
        owner = index // slots
        slot = index % slots
        r, c = owner // 3, owner % 3
        top = info[r, c, 0, slot] + (r - 1) * tile + half
        left = info[r, c, 0, slots + slot] + (c - 1) * tile + half
        live = info[r, c, 0, 2 * slots]
        hit = (slot < live) & (top > 0) & (top < size + tile) & (left > 0) & (left < size + tile)

        @pl.when(hit)
        def _():
            add_window(acc, 0, top, left, power[...])

        return carry

    lax.fori_loop(0, 9 * slots, body, 0)


def project_kernel(tile, half, info, *refs):
    dual, ext, probe, amp, wt, tw = refs[:6]
    base, acc, weight, heavy, power, strips = refs[6:]
    slots = dual.shape[1]
    size = 2 * half
    acc[...] = jnp.zeros_like(acc)
    heavy[...] = jnp.full_like(heavy, BETA)
    power[...] = probe[0] * probe[0] + probe[1] * probe[1]
    add_weights(tile, half, slots, info, heavy, power)
    weight[...] = heavy[0, size : size + tile, size : size + tile]
    live = info[1, 1, 0, 2 * slots]

    def skip(slot, carry):
        base[:, slot] = dual[:, slot]
        return carry

    def many(slots_at):
        tops = [info[1, 1, 0, at] for at in slots_at]
        lefts = [info[1, 1, 0, slots + at] for at in slots_at]
        fh, fl, ih, il = wt[0], wt[1], wt[2], wt[3]
        cr, sr = tw[0], tw[1]
        cc = jnp.broadcast_to(tw[2, :1, :half], (size, half))
        sc = jnp.broadcast_to(tw[2, :1, half:], (size, half))
        n = range(len(slots_at))
        x = []
        for at, top, left in zip(slots_at, tops, lefts):
            pr, pi = probe[0], probe[1]
            wr = load_window(ext, 0, top, left, size)
            wi = load_window(ext, 1, top, left, size)
            re = pr * wr - pi * wi + dual[0, at]
            im = pr * wi + pi * wr + dual[1, at]
            dr, di = re[:half] - re[half:], im[:half] - im[half:]
            x.append(
                cat(
                    [
                        cat([re[:half] + re[half:], dr * cr + di * sr], 1),
                        cat([im[:half] + im[half:], di * cr - dr * sr], 1),
                    ],
                    0,
                )
            )
        y = left_dot(fh, fl, cat(x, 1))
        y = [y[:, 2 * size * i : 2 * size * (i + 1)] for i in n]
        x = []
        for v in y:
            re = cat([v[:half, :size], v[:half, size:]], 0)
            im = cat([v[half:, :size], v[half:, size:]], 0)
            dr, di = re[:, :half] - re[:, half:], im[:, :half] - im[:, half:]
            x.append(cat([re[:, :half] + re[:, half:], im[:, :half] + im[:, half:]], 1))
            x.append(cat([dr * cc + di * sc, di * cc - dr * sc], 1))
        s = right_dot(cat(x, 0), ih, il)
        s = [s[2 * size * i : 2 * size * (i + 1)] for i in n]
        rows = []
        for i, at in enumerate(slots_at):
            for c in range(size // LANES):
                strips[i, c] = amp[at, :, c * LANES : (c + 1) * LANES]
            for first in range(2):
                rows.append(cat([strips[i, c, pl.ds(first, half, stride=2), :] for c in range(size // LANES)], 1))
        ah, al = split(cat(rows, 0))
        a = dot(ah, wt[4]) + dot(al, wt[4])
        x = []
        for i in n:
            b = a[size * i : size * (i + 1)]
            b = cat([b[:, :half], b[:, half:]], 0)
            re, im = s[i][:, :half], s[i][:, half:]
            fac = b * lax.rsqrt(jnp.maximum(re * re + im * im, FLOOR * FLOOR))
            x.append(cat([re * fac, im * fac], 1))
        z = right_dot(cat(x, 0), fh, fl)
        x = []
        for i in n:
            v = z[2 * size * i : 2 * size * (i + 1)]
            er, ei = v[:size, :half], v[:size, half:]
            our, oui = v[size:, :half], v[size:, half:]
            tr, ti = our * cc - oui * sc, oui * cc + our * sc
            re = cat([er + tr, er - tr], 1)
            im = cat([ei + ti, ei - ti], 1)
            x.append(cat([cat([re[:half], re[half:]], 1), cat([im[:half], im[half:]], 1)], 0))
        y = left_dot(ih, il, cat(x, 1))
        for i, (at, top, left) in enumerate(zip(slots_at, tops, lefts)):
            v = y[:, 2 * size * i : 2 * size * (i + 1)]
            er, ei = v[:half, :size], v[half:, :size]
            our, oui = v[:half, size:], v[half:, size:]
            tr, ti = our * cr - oui * sr, oui * cr + our * sr
            dr = cat([er + tr, er - tr], 0) - dual[0, at]
            di = cat([ei + ti, ei - ti], 0) - dual[1, at]
            base[0, at] = -dr
            base[1, at] = -di
            pr, pi = probe[0], probe[1]
            add_window(acc, 0, top, left, pr * dr + pi * di)
            add_window(acc, 1, top, left, pr * di - pi * dr)

    def pair(index, carry):
        many([2 * index, 2 * index + 1])
        return carry

    lax.fori_loop(live, slots, skip, 0)
    lax.fori_loop(0, live // 2, pair, 0)

    @pl.when(live % 2 == 1)
    def _():
        many([live - 1])


def dual_kernel(tile, half, info, ext, probe, base, out, new, ready, sems):
    slots = base.shape[1]
    size = 2 * half
    keep = pltpu.make_async_copy(ext.at[:, half : half + tile, half : half + tile], new, sems.at[slots])
    keep.start()
    copies = []
    for slot in range(slots):
        copy = pltpu.make_async_copy(ready.at[slot], out.at[:, slot], sems.at[slot])
        copies.append(copy)
        active = slot < info[1, 1, 0, 2 * slots]

        @pl.when(jnp.logical_not(active))
        def _():
            ready[slot] = base[:, slot]

        @pl.when(active)
        def _():
            top = info[1, 1, 0, slot]
            left = info[1, 1, 0, slots + slot]
            pr, pi = probe[0], probe[1]
            sr = load_window(ext, 0, top, left, size)
            si = load_window(ext, 1, top, left, size)
            ready[slot, 0] = base[0, slot] + (pr * sr - pi * si)
            ready[slot, 1] = base[1, slot] + (pr * si + pi * sr)

        copy.start()
    for copy in copies:
        copy.wait()
    keep.wait()


def shards(object_field, probe, dual, amplitude, offsets, live):
    tile = object_field.shape[1]
    size = probe.shape[1]
    half = size // 2
    slots = dual.shape[3]
    wide = tile + size
    mid = tile - size
    amps = amplitude.reshape(slots, size, size)
    sd = lambda *shape: jax.ShapeDtypeStruct(shape, F32)
    dma = lambda n: pltpu.SemaphoreType.DMA((n,))
    wt, tw = tables(size)
    fixed = lambda x: pltpu.with_memory_space_constraint(x, pltpu.HBM)

    frame, infos, lam, wt = pl.pallas_call(
        functools.partial(halo_kernel, tile, half),
        out_shape=(
            sd(2, wide, wide),
            jax.ShapeDtypeStruct((3, 3, ROWS, LANES), jnp.int32),
            sd(2, slots, size, size),
            jax.ShapeDtypeStruct(wt.shape, wt.dtype),
        ),
        in_specs=[SM, SM, HBM, HBM, HBM],
        out_specs=(VM, VM, VM, VM),
        scratch_shapes=[
            pltpu.VMEM((ROWS, LANES), jnp.int32),
            pltpu.VMEM((2, mid // 2, half), F32),
            pltpu.VMEM((2, mid // 2, half), F32),
            pltpu.VMEM((2, half, half), F32),
            dma(40),
            dma(40),
            dma(3),
        ],
        compiler_params=pltpu.CompilerParams(collective_id=0, has_side_effects=True, vmem_limit_bytes=16 * MIB),
        cost_estimate=pl.CostEstimate(flops=0, bytes_accessed=80_000_000, transcendentals=0),
        name="halo",
    )(offsets, live, fixed(object_field), fixed(dual.reshape(2, slots, size, size)), fixed(wt))

    cost = lambda size: pl.CostEstimate(flops=0, bytes_accessed=size, transcendentals=0)
    base, acc, weight = pl.pallas_call(
        functools.partial(project_kernel, tile, half),
        out_shape=(sd(2, slots, size, size), sd(2, wide, wide), sd(tile, tile)),
        in_specs=[SM] + [VM] * 6,
        out_specs=(VM, VM, VM),
        scratch_shapes=[
            pltpu.VMEM((1, tile + 2 * size, tile + 2 * size), F32),
            pltpu.VMEM((size, size), F32),
            pltpu.VMEM((2, size // LANES, size, LANES), F32),
        ],
        compiler_params=pltpu.CompilerParams(vmem_limit_bytes=20 * MIB),
        cost_estimate=cost(30_000_000),
        name="project",
    )(infos, lam, frame, probe, amps, wt, tw)

    strip, side, end, via = (2, half, wide), (2, mid, half), (2, 2, half, half), (3, 2, max(half, mid // 2), half)
    frame = pl.pallas_call(
        functools.partial(update_kernel, tile, half),
        out_shape=sd(2, wide, wide),
        in_specs=[VM] * 3,
        out_specs=VM,
        scratch_shapes=[pltpu.VMEM(x, F32) for x in (strip, strip, side, side, end, end, end, end, via, via)] + [dma(60), dma(60)],
        compiler_params=pltpu.CompilerParams(collective_id=1, has_side_effects=True, vmem_limit_bytes=8 * MIB),
        cost_estimate=cost(150_000_000),
        name="update",
    )(acc, object_field, weight)

    dual_new, new = pl.pallas_call(
        functools.partial(dual_kernel, tile, half),
        out_shape=(sd(2, slots, size, size), sd(2, tile, tile)),
        in_specs=[SM, VM, VM, VM],
        out_specs=(ANY, ANY),
        scratch_shapes=[pltpu.VMEM((slots, 2, size, size), F32), dma(slots + 1)],
        compiler_params=pltpu.CompilerParams(vmem_limit_bytes=12 * MIB),
        name="renew",
    )(infos, frame, probe, base)
    return new, dual_new.reshape(dual.shape)


def solution(mesh):
    placed = (
        P(None, "row", "col"),
        P(),
        P(None, "row", "col", None, None, None),
        P("row", "col", None, None, None),
        P(None, "row", "col", None),
        P("row", "col"),
    )
    return jax.shard_map(
        shards,
        mesh=mesh,
        in_specs=placed,
        out_specs=(P(None, "row", "col"), P(None, "row", "col", None, None, None)),
        check_vma=False,
    )
```

```python
import functools
import math

import jax
import jax.numpy as jnp
import numpy as np
from jax import lax
from jax.experimental import pallas as pl
from jax.experimental.pallas import tpu as pltpu
from jax.sharding import PartitionSpec as P

FLOOR = 0.1
BETA = 1.0
LANES = 128
ROWS = 8
MIB = 1 << 20
F32 = jnp.float32
BF16 = jnp.bfloat16
ANY = pl.BlockSpec(memory_space=pl.ANY)
VM = pl.BlockSpec(memory_space=pltpu.VMEM)
SM = pl.BlockSpec(memory_space=pltpu.SMEM)
HBM = pl.BlockSpec(memory_space=pltpu.HBM)


def tables(size):
    n = size // 2
    k = np.arange(n)
    angle = 2.0 * math.pi * ((k[:, None] * k[None, :]) % n) / n
    c, s = np.cos(angle) / math.sqrt(size), np.sin(angle) / math.sqrt(size)
    fwd = np.block([[c, s], [-s, c]])
    inv = np.block([[c, -s], [s, c]])
    parts = []
    for full in (fwd, inv):
        hi = full.astype(np.float32).astype(BF16)
        parts += [hi, (full - hi.astype(np.float64)).astype(np.float32).astype(BF16)]
    perm = np.zeros((size, size), np.float32)
    perm[2 * k, k] = 1.0
    perm[2 * k + 1, n + k] = 1.0
    tw = 2.0 * math.pi * k / size
    ct, st = np.cos(tw).astype(np.float32), np.sin(tw).astype(np.float32)
    rows = np.stack([np.broadcast_to(ct[:, None], (n, size)), np.broadcast_to(st[:, None], (n, size))])
    both = np.broadcast_to(np.concatenate([ct, st])[None, :], (n, size))
    waves = np.concatenate([rows, both[None]]).astype(np.float32)
    return [jnp.asarray(np.stack(parts + [perm.astype(BF16)])), jnp.asarray(waves)]


def split(x):
    hi = x.astype(BF16)
    return hi, (x - hi.astype(F32)).astype(BF16)


def dot(a, b):
    return jnp.dot(a, b, preferred_element_type=F32)


def left_dot(wh, wl, x):
    xh, xl = split(x)
    return dot(wl, xh) + dot(wh, xl) + dot(wh, xh)


def right_dot(x, wh, wl):
    xh, xl = split(x)
    return dot(xh, wl) + dot(xl, wh) + dot(xh, wh)


def cat(parts, axis):
    return jnp.concatenate(parts, axis=axis)


def load_window(ext, channel, top, left, size):
    row = pl.multiple_of((top // ROWS) * ROWS, ROWS)
    base = pl.multiple_of((left // LANES) * LANES, LANES)
    width, height = size + LANES, size + ROWS
    wide = ext[channel, pl.ds(row, height), pl.ds(base, width)]
    wide = pltpu.roll(wide, (width - (left - base)) % width, 1)[:, :size]
    return pltpu.roll(wide, (height - (top - row)) % height, 0)[:size]


def add_window(acc, channel, top, left, value):
    size = value.shape[0]
    row = pl.multiple_of((top // ROWS) * ROWS, ROWS)
    base = pl.multiple_of((left // LANES) * LANES, LANES)
    width, height = size + LANES, size + ROWS
    wide = cat([value, jnp.zeros((ROWS, size), F32)], 0)
    wide = pltpu.roll(wide, top - row, 0)
    wide = cat([wide, jnp.zeros((height, LANES), F32)], 1)
    wide = pltpu.roll(wide, left - base, 1)
    acc[channel, pl.ds(row, height), pl.ds(base, width)] += wide


def clear_beyond(grid, tile, half, frame):
    end = half + tile
    strips = (
        ("up", slice(0, half), slice(None)),
        ("down", slice(end, None), slice(None)),
        ("left", slice(half, end), slice(0, half)),
        ("right", slice(half, end), slice(end, None)),
    )
    for side, rows, cols in strips:

        @pl.when(jnp.logical_not(grid.has[side]))
        def _():
            frame[:, rows, cols] = jnp.zeros_like(frame[:, rows, cols])

    for up, rows in (("up", slice(0, half)), ("down", slice(end, None))):
        for side, cols in (("left", slice(0, half)), ("right", slice(end, None))):

            @pl.when(grid.has[up] & jnp.logical_not(grid.has[side]))
            def _():
                frame[:, rows, cols] = jnp.zeros_like(frame[:, rows, cols])


CHUNKS = 4


class Grid:
    def __init__(self, send, recv):
        row, col = lax.axis_index("row"), lax.axis_index("col")
        self.col, self.cols = col, lax.axis_size("col")
        self.has = {
            "up": row > 0,
            "down": row < lax.axis_size("row") - 1,
            "left": col > 0,
            "right": col < self.cols - 1,
        }
        self.peer = {"up": {"row": row - 1}, "down": {"row": row + 1}, "left": {"col": col - 1}, "right": {"col": col + 1}}
        self.back = {"up": "down", "down": "up", "left": "right", "right": "left"}
        self.step = {"left": -1, "right": 1}
        self.send, self.recv = send, recv
        self.count = 0

    def bends(self):
        return self.cols % 2 == 0 and self.cols > 2

    def relayed(self, col, side, rank):
        gaps = self.cols // 2 - 1
        if side == "right":
            share = CHUNKS * (gaps - col // 2) // (gaps + 1)
            return (col % 2 == 1) & (col > 0) & (col < self.cols - 1) & (rank < share)
        share = CHUNKS * (col // 2) // (gaps + 1)
        return (col % 2 == 0) & (col > 0) & (col < self.cols) & (rank < share)

    def greet(self):
        barrier = pltpu.get_barrier_semaphore()
        col = self.col
        signals = [(self.has[side], self.peer[side]) for side in self.has]
        waits = sum(h.astype(jnp.int32) for h in self.has.values())
        if self.bends():
            signals.append((self.relayed(col - 1, "right", 0), {"col": col - 2}))
            signals.append((self.relayed(col + 1, "left", 0), {"col": col + 2}))
            waits += self.relayed(col + 1, "right", 0).astype(jnp.int32)
            waits += self.relayed(col - 1, "left", 0).astype(jnp.int32)
        for goes, peer in signals:

            @pl.when(goes)
            def _():
                pl.semaphore_signal(barrier, inc=1, device_id=peer, device_id_type=pl.DeviceIdType.MESH)

        pl.semaphore_wait(barrier, waits)

    def copy(self, peer, src, dst):
        at = self.count
        self.count += 1
        return pltpu.make_async_remote_copy(
            src_ref=src,
            dst_ref=dst,
            send_sem=self.send.at[at],
            recv_sem=self.recv.at[at],
            device_id=peer,
            device_id_type=pl.DeviceIdType.MESH,
        )

    def message(self, side, src, dst, also=None):
        goes, comes = self.has[side], self.has[self.back[side]]
        if also is not None:
            goes, comes = goes & self.has[also], comes & self.has[also]
        return self.copy(self.peer[side], src, dst), goes, comes

    def strip(self, side, rank, src, dst, relay):
        return Strip(self, side, rank, src, dst, relay)


class Strip:
    def __init__(self, grid, side, rank, src, dst, relay):
        step, col = grid.step[side], grid.col
        goes, comes = grid.has[side], grid.has[grid.back[side]]
        self.hops = []
        if grid.bends() and relay is not None:
            first, then, last = (grid.relayed(col + step * at, side, rank) for at in (0, 1, -1))
            goes, comes = goes & jnp.logical_not(first), comes & jnp.logical_not(last)
            self.hops.append((grid.copy({"col": col - step}, src, relay), first, then))
            self.hops.append((grid.copy({"col": col + 2 * step}, relay, dst), then, last))
        self.direct = grid.copy(grid.peer[side], src, dst), goes, comes

    def begin(self):
        start(*self.hops[:1])

    def begun(self):
        leave(*self.hops[:1])

    def rest(self):
        start(self.direct)

    def start(self):
        self.begin()
        self.rest()

    def forward(self):
        if self.hops:
            (first, _, comes), (then, _, _) = self.hops

            @pl.when(comes)
            def _():
                first.wait_recv()
                then.start()

    def arrive(self):
        arrive(*self.hops[1:], self.direct)

    def leave(self):
        leave(*self.hops[1:], self.direct)


def when(cond, act):
    if cond is True:
        act()
    else:
        pl.when(cond)(act)


def start(*messages):
    for m in messages:
        if isinstance(m, Strip):
            m.start()
        else:
            pl.when(m[1])(m[0].start)


def each(act, *strips):
    for m in strips:
        getattr(m, act)()


def forward(*strips):
    each("forward", *strips)


def arrive(*messages):
    for m in messages:
        if isinstance(m, Strip):
            m.arrive()
        else:
            pl.when(m[2])(m[0].wait_recv)


def leave(*messages):
    for m in messages:
        if isinstance(m, Strip):
            m.leave()
        else:
            pl.when(m[1])(m[0].wait_send)


def column_messages(grid, tile, half, src, frame, relay):
    size, end = 2 * half, half + tile
    mid = (tile - size) // 2
    rows = [slice(half, half + mid), slice(half + mid, tile - half), slice(0, half), slice(tile - half, tile)]
    groups = []
    for rank, at in enumerate(rows):
        store = slice(at.start + half, at.stop + half)
        via = relay[rank] if rank < len(relay) else None
        groups.append(
            [
                grid.strip("left", rank, src.at[:, at, :half], frame.at[:, store, end:], via),
                grid.strip("right", rank, src.at[:, at, tile - half :], frame.at[:, store, :half], via),
            ]
        )
    return groups[2] + groups[3], groups[0] + groups[1]


def row_messages(grid, tile, half, src, frame):
    end = half + tile
    return [
        grid.message("up", src.at[:, :half, :], frame.at[:, end:, half:end]),
        grid.message("down", src.at[:, tile - half :, :], frame.at[:, :half, half:end]),
    ]


def corner_messages(grid, tile, half, frame):
    size, end = 2 * half, half + tile
    out = []
    for side, cols in (("left", slice(0, half)), ("right", slice(end, None))):
        out.append(grid.message("up", frame.at[:, half:size, cols], frame.at[:, end:, cols], also=side))
        out.append(grid.message("down", frame.at[:, tile:end, cols], frame.at[:, :half, cols], also=side))
    return out


def one_hot(shape, shift):
    gap = lax.broadcasted_iota(jnp.int32, shape, 0) - lax.broadcasted_iota(jnp.int32, shape, 1)
    return jnp.where(gap == shift, 1.0, 0.0).astype(BF16)


def spread_power(tile, half, slots, infos, probe, weight):
    size = 2 * half
    weight[...] = jnp.full_like(weight, BETA)
    high, low = split(probe[0] * probe[0] + probe[1] * probe[1])
    spans = [
        (slice(0, half), slice(half, size), -tile),
        (slice(0, tile), slice(0, size), 0),
        (slice(tile - half, tile), slice(0, half), tile),
    ]
    for r, (rows, along, row_at) in enumerate(spans):
        for c, (cols, across, col_at) in enumerate(spans):
            ny, nk = rows.stop - rows.start, along.stop - along.start
            nx, nl = cols.stop - cols.start, across.stop - across.start
            part = cat([high[along, across], low[along, across]], 0)
            total = weight[rows, cols]
            for slot in range(slots):
                used = slot < infos[r, c, :1, 2 * slots : 2 * slots + 1]
                top = infos[r, c, :1, slot : slot + 1] + (row_at - half - rows.start + along.start)
                left = infos[r, c, :1, slots + slot : slots + slot + 1] + (col_at - half - cols.start + across.start)
                top = jnp.where(used, top, 2 * tile)
                moved = dot(part, one_hot((nl, nx), -left)).astype(BF16)
                place = one_hot((ny, nk), top)
                total = total + dot(place, moved[:nk]) + dot(place, moved[nk:])
            weight[rows, cols] = total


def halo_kernel(tile, half, offsets, live, cells, dual, wt, probe, *refs):
    frame, infos, lam, tables_out, probe_out, weight, acc = refs[:7]
    tag, r0, r1, r2, send, recv, local = refs[7:]
    grid = Grid(send, recv)
    has = grid.has
    slots = offsets.shape[3]
    loads = [
        pltpu.make_async_copy(probe, probe_out, local.at[0]),
        pltpu.make_async_copy(cells, frame.at[:, half : half + tile, half : half + tile], local.at[1]),
        pltpu.make_async_copy(dual, lam, local.at[2]),
        pltpu.make_async_copy(wt, tables_out, local.at[3]),
    ]
    lane = lax.broadcasted_iota(jnp.int32, tag.shape, 1)
    value = jnp.where(lane == 2 * slots, live[0, 0], 0)
    for k in range(slots):
        value = jnp.where(lane == k, offsets[0, 0, 0, k], value)
        value = jnp.where(lane == slots + k, offsets[1, 0, 0, k], value)
    tag[...] = value
    infos[1, 1] = value
    ends, inner = column_messages(grid, tile, half, cells, frame, (r0, r1, r2))
    rows = row_messages(grid, tile, half, cells, frame)
    corners = corner_messages(grid, tile, half, frame)
    tags = [
        grid.message("left", tag, infos.at[1, 2]),
        grid.message("right", tag, infos.at[1, 0]),
    ]
    bands = [
        grid.message("up", infos.at[1], infos.at[2]),
        grid.message("down", infos.at[1], infos.at[0]),
    ]
    grid.greet()
    start(*tags)
    each("begin", *inner, *ends)
    each("rest", *ends)
    start(*rows)
    for copy in loads:
        copy.start()
    clear_beyond(grid, tile, half, frame)
    for side, at in (("left", (1, 0)), ("right", (1, 2)), ("up", (0,)), ("down", (2,))):

        @pl.when(jnp.logical_not(has[side]))
        def _():
            infos[at] = jnp.zeros_like(infos[at])

    arrive(*tags)
    start(*bands)
    each("begun", *inner, *ends)
    each("rest", *inner)
    forward(*inner, *ends)
    loads[0].wait()
    arrive(*bands)
    acc[...] = jnp.zeros_like(acc)
    spread_power(tile, half, slots, infos, probe_out, weight)
    arrive(*ends)
    start(*corners)
    arrive(*inner, *rows, *corners)
    for copy in loads[1:]:
        copy.wait()
    leave(*tags, *ends, *inner, *rows, *bands, *corners)


def update_kernel(tile, half, *refs):
    acc, cells, weight, frame = refs[:4]
    fa, fb, g_lm, g_rm, g_le, g_re, s_le, s_re, sums, news, send, recv = refs[4:]
    size, end = 2 * half, half + tile
    grid = Grid(send, recv)
    has = grid.has
    val = frame.at[:, half:end, half:end]
    up = grid.message("up", acc.at[:, :half, :], fb)
    down = grid.message("down", acc.at[:, end:, :], fa)
    mid = (tile - size) // 2
    mids = []
    for rank in range(2):
        at, to = slice(size + rank * mid, size + (rank + 1) * mid), slice(rank * mid, (rank + 1) * mid)
        mids.append(grid.strip("left", rank, acc.at[:, at, :half], g_rm.at[:, to], sums.at[rank, :, :mid]))
        mids.append(grid.strip("right", rank, acc.at[:, at, end:], g_lm.at[:, to], sums.at[rank, :, :mid]))
    ends = []
    for at in range(2):
        via = sums.at[2] if at == 0 else None
        ends.append(grid.strip("left", 2 + at, s_le.at[:, at], g_re.at[:, at], via))
        ends.append(grid.strip("right", 2 + at, s_re.at[:, at], g_le.at[:, at], via))
    via = [news.at[0, :, :mid], news.at[1, :, :mid], news.at[2]]
    new_ends, new_inner = column_messages(grid, tile, half, val, frame, via)
    new_rows = row_messages(grid, tile, half, val, frame)
    corners = corner_messages(grid, tile, half, frame)
    grid.greet()
    each("begin", *mids)
    start(up, down)
    each("rest", *mids)
    clear_beyond(grid, tile, half, frame)
    for side, buffers in (("up", (fa,)), ("down", (fb,)), ("left", (g_lm, g_le)), ("right", (g_rm, g_re))):

        @pl.when(jnp.logical_not(has[side]))
        def _():
            for b in buffers:
                b[...] = jnp.zeros_like(b)

    arrive(up, down)
    for ch in range(2):
        s_le[ch, 0] = acc[ch, half:size, :half] + fa[ch, :, :half]
        s_le[ch, 1] = acc[ch, tile:end, :half] + fb[ch, :, :half]
        s_re[ch, 0] = acc[ch, half:size, end:] + fa[ch, :, end:]
        s_re[ch, 1] = acc[ch, tile:end, end:] + fb[ch, :, end:]
    start(*ends)
    tops, bottoms, inner = slice(0, half), slice(tile - half, tile), slice(half, tile - half)
    heads, tails = slice(0, half), slice(tile - half, tile)

    def moved(at):
        return slice(at.start + half, at.stop + half)

    def settle(ch, rows, cols, more):
        total = acc[ch, moved(rows), moved(cols)] + BETA * cells[ch, rows, cols]
        for m in more:
            total = total + m
        frame[ch, moved(rows), moved(cols)] = total / weight[rows, cols]

    forward(*mids)
    for ch in range(2):
        settle(ch, inner, inner, ())
        settle(ch, tops, inner, (fa[ch, :, size:tile],))
        settle(ch, bottoms, inner, (fb[ch, :, size:tile],))
    arrive(*mids)
    for ch in range(2):
        settle(ch, inner, heads, (g_lm[ch],))
        settle(ch, inner, tails, (g_rm[ch],))
    first, second = [], new_inner
    forward(*ends)
    arrive(*ends)
    for ch in range(2):
        settle(ch, tops, heads, (fa[ch, :, half:size], g_le[ch, 0]))
        settle(ch, bottoms, heads, (fb[ch, :, half:size], g_le[ch, 1]))
        settle(ch, tops, tails, (fa[ch, :, tile:end], g_re[ch, 0]))
        settle(ch, bottoms, tails, (fb[ch, :, tile:end], g_re[ch, 1]))
    each("begin", *new_ends, *second)
    each("rest", *new_ends)
    start(*new_rows)
    forward(*first)
    each("begun", *new_ends, *second)
    each("rest", *second)
    forward(*new_ends, *second)
    arrive(*new_ends)
    start(*corners)
    arrive(*new_inner, *new_rows, *corners)
    each("begun", *mids, *ends, *first)
    leave(up, down, *mids, *ends, *new_ends, *new_inner, *new_rows, *corners)


def project_kernel(tile, half, info, *refs):
    dual, ext, probe, amp, wt, tw = refs[:6]
    base, acc, strips = refs[7:]
    slots = dual.shape[1]
    size = 2 * half
    live = info[1, 1, 0, 2 * slots]

    def skip(slot, carry):
        base[:, slot] = dual[:, slot]
        return carry

    def many(slots_at):
        tops = [info[1, 1, 0, at] for at in slots_at]
        lefts = [info[1, 1, 0, slots + at] for at in slots_at]
        fh, fl, ih, il = wt[0], wt[1], wt[2], wt[3]
        cr, sr = tw[0], tw[1]
        cc = jnp.broadcast_to(tw[2, :1, :half], (size, half))
        sc = jnp.broadcast_to(tw[2, :1, half:], (size, half))
        n = range(len(slots_at))
        x = []
        for at, top, left in zip(slots_at, tops, lefts):
            pr, pi = probe[0], probe[1]
            wr = load_window(ext, 0, top, left, size)
            wi = load_window(ext, 1, top, left, size)
            re = pr * wr - pi * wi + dual[0, at]
            im = pr * wi + pi * wr + dual[1, at]
            dr, di = re[:half] - re[half:], im[:half] - im[half:]
            x.append(
                cat(
                    [
                        cat([re[:half] + re[half:], dr * cr + di * sr], 1),
                        cat([im[:half] + im[half:], di * cr - dr * sr], 1),
                    ],
                    0,
                )
            )
        y = left_dot(fh, fl, cat(x, 1))
        y = [y[:, 2 * size * i : 2 * size * (i + 1)] for i in n]
        x = []
        for v in y:
            re = cat([v[:half, :size], v[:half, size:]], 0)
            im = cat([v[half:, :size], v[half:, size:]], 0)
            dr, di = re[:, :half] - re[:, half:], im[:, :half] - im[:, half:]
            x.append(cat([re[:, :half] + re[:, half:], im[:, :half] + im[:, half:]], 1))
            x.append(cat([dr * cc + di * sc, di * cc - dr * sc], 1))
        s = right_dot(cat(x, 0), ih, il)
        s = [s[2 * size * i : 2 * size * (i + 1)] for i in n]
        rows = []
        for i, at in enumerate(slots_at):
            for c in range(size // LANES):
                strips[i, c] = amp[at, :, c * LANES : (c + 1) * LANES]
            for first in range(2):
                rows.append(cat([strips[i, c, pl.ds(first, half, stride=2), :] for c in range(size // LANES)], 1))
        ah, al = split(cat(rows, 0))
        a = dot(ah, wt[4]) + dot(al, wt[4])
        x = []
        for i in n:
            b = a[size * i : size * (i + 1)]
            b = cat([b[:, :half], b[:, half:]], 0)
            re, im = s[i][:, :half], s[i][:, half:]
            fac = b * lax.rsqrt(jnp.maximum(re * re + im * im, FLOOR * FLOOR))
            x.append(cat([re * fac, im * fac], 1))
        z = right_dot(cat(x, 0), fh, fl)
        x = []
        for i in n:
            v = z[2 * size * i : 2 * size * (i + 1)]
            er, ei = v[:size, :half], v[:size, half:]
            our, oui = v[size:, :half], v[size:, half:]
            tr, ti = our * cc - oui * sc, oui * cc + our * sc
            re = cat([er + tr, er - tr], 1)
            im = cat([ei + ti, ei - ti], 1)
            x.append(cat([cat([re[:half], re[half:]], 1), cat([im[:half], im[half:]], 1)], 0))
        y = left_dot(ih, il, cat(x, 1))
        for i, (at, top, left) in enumerate(zip(slots_at, tops, lefts)):
            v = y[:, 2 * size * i : 2 * size * (i + 1)]
            er, ei = v[:half, :size], v[half:, :size]
            our, oui = v[:half, size:], v[half:, size:]
            tr, ti = our * cr - oui * sr, oui * cr + our * sr
            dr = cat([er + tr, er - tr], 0) - dual[0, at]
            di = cat([ei + ti, ei - ti], 0) - dual[1, at]
            base[0, at] = -dr
            base[1, at] = -di
            pr, pi = probe[0], probe[1]
            add_window(acc, 0, top, left, pr * dr + pi * di)
            add_window(acc, 1, top, left, pr * di - pi * dr)

    def pair(index, carry):
        many([2 * index, 2 * index + 1])
        return carry

    lax.fori_loop(live, slots, skip, 0)
    lax.fori_loop(0, live // 2, pair, 0)

    @pl.when(live % 2 == 1)
    def _():
        many([live - 1])


def dual_kernel(tile, half, info, ext, probe, base, out, new, ready, sems):
    slots = base.shape[1]
    size = 2 * half
    keep = pltpu.make_async_copy(ext.at[:, half : half + tile, half : half + tile], new, sems.at[slots])
    keep.start()
    copies = []
    for slot in range(slots):
        copy = pltpu.make_async_copy(ready.at[slot], out.at[:, slot], sems.at[slot])
        copies.append(copy)
        active = slot < info[1, 1, 0, 2 * slots]

        @pl.when(jnp.logical_not(active))
        def _():
            ready[slot] = base[:, slot]

        @pl.when(active)
        def _():
            top = info[1, 1, 0, slot]
            left = info[1, 1, 0, slots + slot]
            pr, pi = probe[0], probe[1]
            sr = load_window(ext, 0, top, left, size)
            si = load_window(ext, 1, top, left, size)
            ready[slot, 0] = base[0, slot] + (pr * sr - pi * si)
            ready[slot, 1] = base[1, slot] + (pr * si + pi * sr)

        copy.start()
    for copy in copies:
        copy.wait()
    keep.wait()


def shards(object_field, probe, dual, amplitude, offsets, live):
    tile = object_field.shape[1]
    size = probe.shape[1]
    half = size // 2
    slots = dual.shape[3]
    wide = tile + size
    mid = tile - size
    amps = amplitude.reshape(slots, size, size)
    sd = lambda *shape: jax.ShapeDtypeStruct(shape, F32)
    dma = lambda n: pltpu.SemaphoreType.DMA((n,))
    wt, tw = tables(size)
    fixed = lambda x: pltpu.with_memory_space_constraint(x, pltpu.HBM)

    frame, infos, lam, wt, probe, weight, acc = pl.pallas_call(
        functools.partial(halo_kernel, tile, half),
        out_shape=(
            sd(2, wide, wide),
            jax.ShapeDtypeStruct((3, 3, ROWS, LANES), jnp.int32),
            sd(2, slots, size, size),
            jax.ShapeDtypeStruct(wt.shape, wt.dtype),
            sd(2, size, size),
            sd(tile, tile),
            sd(2, wide, wide),
        ),
        in_specs=[SM, SM, HBM, HBM, HBM, HBM],
        out_specs=(VM,) * 7,
        scratch_shapes=[
            pltpu.VMEM((ROWS, LANES), jnp.int32),
            pltpu.VMEM((2, mid // 2, half), F32),
            pltpu.VMEM((2, mid // 2, half), F32),
            pltpu.VMEM((2, half, half), F32),
            dma(40),
            dma(40),
            dma(4),
        ],
        compiler_params=pltpu.CompilerParams(collective_id=0, has_side_effects=True, vmem_limit_bytes=16 * MIB),
        cost_estimate=pl.CostEstimate(flops=0, bytes_accessed=80_000_000, transcendentals=0),
        name="halo",
    )(offsets, live, fixed(object_field), fixed(dual.reshape(2, slots, size, size)), fixed(wt), fixed(probe))

    cost = lambda size: pl.CostEstimate(flops=0, bytes_accessed=size, transcendentals=0)
    base, acc = pl.pallas_call(
        functools.partial(project_kernel, tile, half),
        out_shape=(sd(2, slots, size, size), sd(2, wide, wide)),
        in_specs=[SM] + [VM] * 7,
        out_specs=(VM, VM),
        input_output_aliases={7: 1},
        scratch_shapes=[pltpu.VMEM((2, size // LANES, size, LANES), F32)],
        compiler_params=pltpu.CompilerParams(vmem_limit_bytes=20 * MIB),
        cost_estimate=cost(30_000_000),
        name="project",
    )(infos, lam, frame, probe, amps, wt, tw, acc)

    strip, side, end, via = (2, half, wide), (2, mid, half), (2, 2, half, half), (3, 2, max(half, mid // 2), half)
    frame = pl.pallas_call(
        functools.partial(update_kernel, tile, half),
        out_shape=sd(2, wide, wide),
        in_specs=[VM] * 3,
        out_specs=VM,
        scratch_shapes=[pltpu.VMEM(x, F32) for x in (strip, strip, side, side, end, end, end, end, via, via)] + [dma(60), dma(60)],
        compiler_params=pltpu.CompilerParams(collective_id=1, has_side_effects=True, vmem_limit_bytes=8 * MIB),
        cost_estimate=cost(150_000_000),
        name="update",
    )(acc, object_field, weight)

    dual_new, new = pl.pallas_call(
        functools.partial(dual_kernel, tile, half),
        out_shape=(sd(2, slots, size, size), sd(2, tile, tile)),
        in_specs=[SM, VM, VM, VM],
        out_specs=(ANY, ANY),
        scratch_shapes=[pltpu.VMEM((slots, 2, size, size), F32), dma(slots + 1)],
        compiler_params=pltpu.CompilerParams(vmem_limit_bytes=12 * MIB),
        name="renew",
    )(infos, frame, probe, base)
    return new, dual_new.reshape(dual.shape)


def solution(mesh):
    placed = (
        P(None, "row", "col"),
        P(),
        P(None, "row", "col", None, None, None),
        P("row", "col", None, None, None),
        P(None, "row", "col", None),
        P("row", "col"),
    )
    return jax.shard_map(
        shards,
        mesh=mesh,
        in_specs=placed,
        out_specs=(P(None, "row", "col"), P(None, "row", "col", None, None, None)),
        check_vma=False,
    )
```

```python
import functools
import math

import jax
import jax.numpy as jnp
import numpy as np
from jax import lax
from jax.experimental import pallas as pl
from jax.experimental.pallas import tpu as pltpu
from jax.sharding import PartitionSpec as P

FLOOR = 0.1
BETA = 1.0
LANES = 128
ROWS = 8
MIB = 1 << 20
F32 = jnp.float32
BF16 = jnp.bfloat16
ANY = pl.BlockSpec(memory_space=pl.ANY)
VM = pl.BlockSpec(memory_space=pltpu.VMEM)
SM = pl.BlockSpec(memory_space=pltpu.SMEM)
HBM = pl.BlockSpec(memory_space=pltpu.HBM)


def tables(size):
    n = size // 2
    k = np.arange(n)
    angle = 2.0 * math.pi * ((k[:, None] * k[None, :]) % n) / n
    c, s = np.cos(angle) / math.sqrt(size), np.sin(angle) / math.sqrt(size)
    fwd = np.block([[c, s], [-s, c]])
    inv = np.block([[c, -s], [s, c]])
    parts = []
    for full in (fwd, inv):
        hi = full.astype(np.float32).astype(BF16)
        parts += [hi, (full - hi.astype(np.float64)).astype(np.float32).astype(BF16)]
    perm = np.zeros((size, size), np.float32)
    perm[2 * k, k] = 1.0
    perm[2 * k + 1, n + k] = 1.0
    tw = 2.0 * math.pi * k / size
    ct, st = np.cos(tw).astype(np.float32), np.sin(tw).astype(np.float32)
    rows = np.stack([np.broadcast_to(ct[:, None], (n, size)), np.broadcast_to(st[:, None], (n, size))])
    both = np.broadcast_to(np.concatenate([ct, st])[None, :], (n, size))
    waves = np.concatenate([rows, both[None]]).astype(np.float32)
    return [jnp.asarray(np.stack(parts + [perm.astype(BF16)])), jnp.asarray(waves)]


def split(x):
    hi = x.astype(BF16)
    return hi, (x - hi.astype(F32)).astype(BF16)


def dot(a, b):
    return jnp.dot(a, b, preferred_element_type=F32)


def left_dot(wh, wl, x):
    xh, xl = split(x)
    return dot(wl, xh) + dot(wh, xl) + dot(wh, xh)


def right_dot(x, wh, wl):
    xh, xl = split(x)
    return dot(xh, wl) + dot(xl, wh) + dot(xh, wh)


def cat(parts, axis):
    return jnp.concatenate(parts, axis=axis)


def load_window(ext, channel, top, left, size):
    row = pl.multiple_of((top // ROWS) * ROWS, ROWS)
    base = pl.multiple_of((left // LANES) * LANES, LANES)
    width, height = size + LANES, size + ROWS
    wide = ext[channel, pl.ds(row, height), pl.ds(base, width)]
    wide = pltpu.roll(wide, (width - (left - base)) % width, 1)[:, :size]
    return pltpu.roll(wide, (height - (top - row)) % height, 0)[:size]


def add_window(acc, channel, top, left, value):
    size = value.shape[0]
    row = pl.multiple_of((top // ROWS) * ROWS, ROWS)
    base = pl.multiple_of((left // LANES) * LANES, LANES)
    width, height = size + LANES, size + ROWS
    wide = cat([value, jnp.zeros((ROWS, size), F32)], 0)
    wide = pltpu.roll(wide, top - row, 0)
    wide = cat([wide, jnp.zeros((height, LANES), F32)], 1)
    wide = pltpu.roll(wide, left - base, 1)
    acc[channel, pl.ds(row, height), pl.ds(base, width)] += wide


def clear_beyond(grid, tile, half, frame):
    end = half + tile
    strips = (
        ("up", slice(0, half), slice(None)),
        ("down", slice(end, None), slice(None)),
        ("left", slice(half, end), slice(0, half)),
        ("right", slice(half, end), slice(end, None)),
    )
    for side, rows, cols in strips:

        @pl.when(jnp.logical_not(grid.has[side]))
        def _():
            frame[:, rows, cols] = jnp.zeros_like(frame[:, rows, cols])

    for up, rows in (("up", slice(0, half)), ("down", slice(end, None))):
        for side, cols in (("left", slice(0, half)), ("right", slice(end, None))):

            @pl.when(grid.has[up] & jnp.logical_not(grid.has[side]))
            def _():
                frame[:, rows, cols] = jnp.zeros_like(frame[:, rows, cols])


CHUNKS = 4


class Grid:
    def __init__(self, send, recv):
        row, col = lax.axis_index("row"), lax.axis_index("col")
        self.col, self.cols = col, lax.axis_size("col")
        self.has = {
            "up": row > 0,
            "down": row < lax.axis_size("row") - 1,
            "left": col > 0,
            "right": col < self.cols - 1,
        }
        self.peer = {"up": {"row": row - 1}, "down": {"row": row + 1}, "left": {"col": col - 1}, "right": {"col": col + 1}}
        self.back = {"up": "down", "down": "up", "left": "right", "right": "left"}
        self.step = {"left": -1, "right": 1}
        self.send, self.recv = send, recv
        self.count = 0

    def bends(self):
        return self.cols % 2 == 0 and self.cols > 2

    def relayed(self, col, side, rank):
        gaps = self.cols // 2 - 1
        if side == "right":
            share = CHUNKS * (gaps - col // 2) // (gaps + 1)
            return (col % 2 == 1) & (col > 0) & (col < self.cols - 1) & (rank < share)
        share = CHUNKS * (col // 2) // (gaps + 1)
        return (col % 2 == 0) & (col > 0) & (col < self.cols) & (rank < share)

    def greet(self, between=None):
        barrier = pltpu.get_barrier_semaphore()
        col = self.col
        signals = [(self.has[side], self.peer[side]) for side in self.has]
        waits = sum(h.astype(jnp.int32) for h in self.has.values())
        if self.bends():
            signals.append((self.relayed(col - 1, "right", 0), {"col": col - 2}))
            signals.append((self.relayed(col + 1, "left", 0), {"col": col + 2}))
            waits += self.relayed(col + 1, "right", 0).astype(jnp.int32)
            waits += self.relayed(col - 1, "left", 0).astype(jnp.int32)
        for goes, peer in signals:

            @pl.when(goes)
            def _():
                pl.semaphore_signal(barrier, inc=1, device_id=peer, device_id_type=pl.DeviceIdType.MESH)

        if between is not None:
            between()
        pl.semaphore_wait(barrier, waits)

    def copy(self, peer, src, dst):
        at = self.count
        self.count += 1
        return pltpu.make_async_remote_copy(
            src_ref=src,
            dst_ref=dst,
            send_sem=self.send.at[at],
            recv_sem=self.recv.at[at],
            device_id=peer,
            device_id_type=pl.DeviceIdType.MESH,
        )

    def message(self, side, src, dst, also=None):
        goes, comes = self.has[side], self.has[self.back[side]]
        if also is not None:
            goes, comes = goes & self.has[also], comes & self.has[also]
        return self.copy(self.peer[side], src, dst), goes, comes

    def strip(self, side, rank, src, dst, relay):
        return Strip(self, side, rank, src, dst, relay)


class Strip:
    def __init__(self, grid, side, rank, src, dst, relay):
        step, col = grid.step[side], grid.col
        goes, comes = grid.has[side], grid.has[grid.back[side]]
        self.hops = []
        if grid.bends() and relay is not None:
            first, then, last = (grid.relayed(col + step * at, side, rank) for at in (0, 1, -1))
            goes, comes = goes & jnp.logical_not(first), comes & jnp.logical_not(last)
            self.hops.append((grid.copy({"col": col - step}, src, relay), first, then))
            self.hops.append((grid.copy({"col": col + 2 * step}, relay, dst), then, last))
        self.direct = grid.copy(grid.peer[side], src, dst), goes, comes

    def begin(self):
        start(*self.hops[:1])

    def begun(self):
        leave(*self.hops[:1])

    def rest(self):
        start(self.direct)

    def start(self):
        self.begin()
        self.rest()

    def forward(self):
        if self.hops:
            (first, _, comes), (then, _, _) = self.hops

            @pl.when(comes)
            def _():
                first.wait_recv()
                then.start()

    def arrive(self):
        arrive(*self.hops[1:], self.direct)

    def leave(self):
        leave(*self.hops[1:], self.direct)


def when(cond, act):
    if cond is True:
        act()
    else:
        pl.when(cond)(act)


def start(*messages):
    for m in messages:
        if isinstance(m, Strip):
            m.start()
        else:
            pl.when(m[1])(m[0].start)


def each(act, *strips):
    for m in strips:
        getattr(m, act)()


def forward(*strips):
    each("forward", *strips)


def arrive(*messages):
    for m in messages:
        if isinstance(m, Strip):
            m.arrive()
        else:
            pl.when(m[2])(m[0].wait_recv)


def leave(*messages):
    for m in messages:
        if isinstance(m, Strip):
            m.leave()
        else:
            pl.when(m[1])(m[0].wait_send)


def column_messages(grid, tile, half, src, frame, relay):
    size, end = 2 * half, half + tile
    mid = (tile - size) // 2
    rows = [slice(half, half + mid), slice(half + mid, tile - half), slice(0, half), slice(tile - half, tile)]
    groups = []
    for rank, at in enumerate(rows):
        store = slice(at.start + half, at.stop + half)
        via = relay[rank] if rank < len(relay) else None
        groups.append(
            [
                grid.strip("left", rank, src.at[:, at, :half], frame.at[:, store, end:], via),
                grid.strip("right", rank, src.at[:, at, tile - half :], frame.at[:, store, :half], via),
            ]
        )
    return groups[2] + groups[3], groups[0] + groups[1]


def row_messages(grid, tile, half, src, frame):
    end = half + tile
    return [
        grid.message("up", src.at[:, :half, :], frame.at[:, end:, half:end]),
        grid.message("down", src.at[:, tile - half :, :], frame.at[:, :half, half:end]),
    ]


def corner_messages(grid, tile, half, frame):
    size, end = 2 * half, half + tile
    out = []
    for side, cols in (("left", slice(0, half)), ("right", slice(end, None))):
        out.append(grid.message("up", frame.at[:, half:size, cols], frame.at[:, end:, cols], also=side))
        out.append(grid.message("down", frame.at[:, tile:end, cols], frame.at[:, :half, cols], also=side))
    return out


def one_hot(shape, shift):
    gap = lax.broadcasted_iota(jnp.int32, shape, 0) - lax.broadcasted_iota(jnp.int32, shape, 1)
    return jnp.where(gap == shift, 1.0, 0.0).astype(BF16)


def spread_power(tile, half, slots, bands, infos, probe, weight):
    size = 2 * half
    high, low = split(probe[0] * probe[0] + probe[1] * probe[1])
    spans = [
        (slice(0, half), slice(half, size), -tile),
        (slice(0, tile), slice(0, size), 0),
        (slice(tile - half, tile), slice(0, half), tile),
    ]
    for r in bands:
        rows, along, row_at = spans[r]
        for c, (cols, across, col_at) in enumerate(spans):
            ny, nk = rows.stop - rows.start, along.stop - along.start
            nx, nl = cols.stop - cols.start, across.stop - across.start
            part = cat([high[along, across], low[along, across]], 0)
            total = weight[rows, cols]
            for slot in range(slots):
                used = slot < infos[r, c, :1, 2 * slots : 2 * slots + 1]
                top = infos[r, c, :1, slot : slot + 1] + (row_at - half - rows.start + along.start)
                left = infos[r, c, :1, slots + slot : slots + slot + 1] + (col_at - half - cols.start + across.start)
                top = jnp.where(used, top, 2 * tile)
                moved = dot(part, one_hot((nl, nx), -left)).astype(BF16)
                place = one_hot((ny, nk), top)
                total = total + dot(place, moved[:nk]) + dot(place, moved[nk:])
            weight[rows, cols] = total


def sort_amplitude(slots, amp, strips, perm, out):
    count, size = strips.shape[0], strips.shape[1]
    half = size // 2
    for slot in range(slots):
        for c in range(count):
            strips[c] = amp[slot, :, c * LANES : (c + 1) * LANES]
        rows = []
        for first in range(2):
            rows.append(cat([strips[c, pl.ds(first, half, stride=2), :] for c in range(count)], 1))
        high, low = split(cat(rows, 0))
        a = dot(high, perm) + dot(low, perm)
        out[slot] = cat([a[:, :half], a[:, half:]], 0)


def halo_kernel(tile, half, places, live, cells, dual, wt, probe, amp, *refs):
    frame, lam, tables_out, probe_out, weight, acc, sorted_amp = refs[:7]
    offsets, infos, tag, plain_amp, strips, r0, r1, r2, send, recv, local = refs[7:]
    grid = Grid(send, recv)
    has = grid.has
    slots = offsets.shape[3]
    scalars = pltpu.make_async_copy(places, offsets, local.at[5])
    scalars.start()
    loads = [
        pltpu.make_async_copy(probe, probe_out, local.at[0]),
        pltpu.make_async_copy(cells, frame.at[:, half : half + tile, half : half + tile], local.at[1]),
        pltpu.make_async_copy(dual, lam, local.at[2]),
        pltpu.make_async_copy(wt, tables_out, local.at[3]),
        pltpu.make_async_copy(amp, plain_amp, local.at[4]),
    ]
    ends, inner = column_messages(grid, tile, half, cells, frame, (r0, r1, r2))
    rows = row_messages(grid, tile, half, cells, frame)
    corners = corner_messages(grid, tile, half, frame)
    tags = [
        grid.message("left", tag, infos.at[1, 2]),
        grid.message("right", tag, infos.at[1, 0]),
    ]
    bands = [
        grid.message("up", infos.at[1], infos.at[2]),
        grid.message("down", infos.at[1], infos.at[0]),
    ]

    def make_tag():
        scalars.wait()
        lane = lax.broadcasted_iota(jnp.int32, tag.shape, 1)
        value = jnp.where(lane == 2 * slots, live[0, 0], 0)
        for k in range(slots):
            value = jnp.where(lane == k, offsets[0, 0, 0, k], value)
            value = jnp.where(lane == slots + k, offsets[1, 0, 0, k], value)
        tag[...] = value
        infos[1, 1] = value

    grid.greet(make_tag)
    start(*tags)
    each("begin", *inner, *ends)
    each("rest", *ends)
    for copy in loads:
        copy.start()
    clear_beyond(grid, tile, half, frame)
    for side, at in (("left", (1, 0)), ("right", (1, 2)), ("up", (0,)), ("down", (2,))):

        @pl.when(jnp.logical_not(has[side]))
        def _():
            infos[at] = jnp.zeros_like(infos[at])

    arrive(*tags)
    start(*bands, *rows)
    each("begun", *inner, *ends)
    each("rest", *inner)
    forward(*inner, *ends)
    loads[0].wait()
    arrive(*bands)
    acc[...] = jnp.zeros_like(acc)
    weight[...] = jnp.full_like(weight, BETA)
    spread_power(tile, half, slots, (0, 2), infos, probe_out, weight)
    arrive(*ends)
    start(*corners)
    spread_power(tile, half, slots, (1,), infos, probe_out, weight)
    for copy in loads[1:]:
        copy.wait()
    sort_amplitude(slots, plain_amp, strips, tables_out[4], sorted_amp)
    arrive(*inner, *rows, *corners)
    leave(*tags, *ends, *inner, *rows, *bands, *corners)


def update_kernel(tile, half, *refs):
    acc, cells, weight, frame = refs[:4]
    fa, fb, g_lm, g_rm, g_le, g_re, s_le, s_re, sums, news, send, recv = refs[4:]
    size, end = 2 * half, half + tile
    grid = Grid(send, recv)
    has = grid.has
    val = frame.at[:, half:end, half:end]
    up = grid.message("up", acc.at[:, :half, :], fb)
    down = grid.message("down", acc.at[:, end:, :], fa)
    mid = (tile - size) // 2
    mids = []
    for rank in range(2):
        at, to = slice(size + rank * mid, size + (rank + 1) * mid), slice(rank * mid, (rank + 1) * mid)
        mids.append(grid.strip("left", rank, acc.at[:, at, :half], g_rm.at[:, to], sums.at[rank, :, :mid]))
        mids.append(grid.strip("right", rank, acc.at[:, at, end:], g_lm.at[:, to], sums.at[rank, :, :mid]))
    ends = []
    for at in range(2):
        via = sums.at[2] if at == 0 else None
        ends.append(grid.strip("left", 2 + at, s_le.at[:, at], g_re.at[:, at], via))
        ends.append(grid.strip("right", 2 + at, s_re.at[:, at], g_le.at[:, at], via))
    via = [news.at[0, :, :mid], news.at[1, :, :mid], news.at[2]]
    new_ends, new_inner = column_messages(grid, tile, half, val, frame, via)
    new_rows = row_messages(grid, tile, half, val, frame)
    corners = corner_messages(grid, tile, half, frame)
    grid.greet()
    each("begin", *mids)
    start(up, down)
    each("rest", *mids)
    clear_beyond(grid, tile, half, frame)
    for side, buffers in (("up", (fa,)), ("down", (fb,)), ("left", (g_lm, g_le)), ("right", (g_rm, g_re))):

        @pl.when(jnp.logical_not(has[side]))
        def _():
            for b in buffers:
                b[...] = jnp.zeros_like(b)

    arrive(up, down)
    for ch in range(2):
        s_le[ch, 0] = acc[ch, half:size, :half] + fa[ch, :, :half]
        s_le[ch, 1] = acc[ch, tile:end, :half] + fb[ch, :, :half]
        s_re[ch, 0] = acc[ch, half:size, end:] + fa[ch, :, end:]
        s_re[ch, 1] = acc[ch, tile:end, end:] + fb[ch, :, end:]
    start(*ends)
    tops, bottoms, inner = slice(0, half), slice(tile - half, tile), slice(half, tile - half)
    heads, tails = slice(0, half), slice(tile - half, tile)

    def moved(at):
        return slice(at.start + half, at.stop + half)

    def settle(ch, rows, cols, more):
        total = acc[ch, moved(rows), moved(cols)] + BETA * cells[ch, rows, cols]
        for m in more:
            total = total + m
        frame[ch, moved(rows), moved(cols)] = total / weight[rows, cols]

    forward(*mids)
    for ch in range(2):
        settle(ch, inner, inner, ())
        settle(ch, tops, inner, (fa[ch, :, size:tile],))
        settle(ch, bottoms, inner, (fb[ch, :, size:tile],))
    arrive(*mids)
    for ch in range(2):
        settle(ch, inner, heads, (g_lm[ch],))
        settle(ch, inner, tails, (g_rm[ch],))
    first, second = [], new_inner
    forward(*ends)
    arrive(*ends)
    for ch in range(2):
        settle(ch, tops, heads, (fa[ch, :, half:size], g_le[ch, 0]))
        settle(ch, bottoms, heads, (fb[ch, :, half:size], g_le[ch, 1]))
        settle(ch, tops, tails, (fa[ch, :, tile:end], g_re[ch, 0]))
        settle(ch, bottoms, tails, (fb[ch, :, tile:end], g_re[ch, 1]))
    each("begin", *new_ends, *second)
    each("rest", *new_ends)
    start(*new_rows)
    forward(*first)
    each("begun", *new_ends, *second)
    each("rest", *second)
    forward(*new_ends, *second)
    arrive(*new_ends)
    start(*corners)
    arrive(*new_inner, *new_rows, *corners)
    each("begun", *mids, *ends, *first)
    leave(up, down, *mids, *ends, *new_ends, *new_inner, *new_rows, *corners)


def project_kernel(tile, half, offsets, count, *refs):
    dual, ext, probe, amp, wt, tw = refs[:6]
    base, acc = refs[7:]
    slots = dual.shape[1]
    size = 2 * half
    live = count[0, 0]

    def skip(slot, carry):
        base[:, slot] = dual[:, slot]
        return carry

    def many(slots_at):
        tops = [offsets[0, 0, 0, at] for at in slots_at]
        lefts = [offsets[1, 0, 0, at] for at in slots_at]
        fh, fl, ih, il = wt[0], wt[1], wt[2], wt[3]
        cr, sr = tw[0], tw[1]
        cc = jnp.broadcast_to(tw[2, :1, :half], (size, half))
        sc = jnp.broadcast_to(tw[2, :1, half:], (size, half))
        n = range(len(slots_at))
        x = []
        for at, top, left in zip(slots_at, tops, lefts):
            pr, pi = probe[0], probe[1]
            wr = load_window(ext, 0, top, left, size)
            wi = load_window(ext, 1, top, left, size)
            re = pr * wr - pi * wi + dual[0, at]
            im = pr * wi + pi * wr + dual[1, at]
            dr, di = re[:half] - re[half:], im[:half] - im[half:]
            x.append(
                cat(
                    [
                        cat([re[:half] + re[half:], dr * cr + di * sr], 1),
                        cat([im[:half] + im[half:], di * cr - dr * sr], 1),
                    ],
                    0,
                )
            )
        y = [left_dot(fh, fl, v) for v in x]
        x = []
        for v in y:
            re = cat([v[:half, :size], v[:half, size:]], 0)
            im = cat([v[half:, :size], v[half:, size:]], 0)
            dr, di = re[:, :half] - re[:, half:], im[:, :half] - im[:, half:]
            x.append(cat([re[:, :half] + re[:, half:], im[:, :half] + im[:, half:]], 1))
            x.append(cat([dr * cc + di * sc, di * cc - dr * sc], 1))
        s = [right_dot(cat(x[2 * i : 2 * i + 2], 0), ih, il) for i in n]
        x = []
        for i, at in enumerate(slots_at):
            b = amp[at]
            re, im = s[i][:, :half], s[i][:, half:]
            fac = b * lax.rsqrt(jnp.maximum(re * re + im * im, FLOOR * FLOOR))
            x.append(cat([re * fac, im * fac], 1))
        z = [right_dot(v, fh, fl) for v in x]
        x = []
        for i in n:
            v = z[i]
            er, ei = v[:size, :half], v[:size, half:]
            our, oui = v[size:, :half], v[size:, half:]
            tr, ti = our * cc - oui * sc, oui * cc + our * sc
            re = cat([er + tr, er - tr], 1)
            im = cat([ei + ti, ei - ti], 1)
            x.append(cat([cat([re[:half], re[half:]], 1), cat([im[:half], im[half:]], 1)], 0))
        y = [left_dot(ih, il, v) for v in x]
        for i, (at, top, left) in enumerate(zip(slots_at, tops, lefts)):
            v = y[i]
            er, ei = v[:half, :size], v[half:, :size]
            our, oui = v[:half, size:], v[half:, size:]
            tr, ti = our * cr - oui * sr, oui * cr + our * sr
            dr = cat([er + tr, er - tr], 0) - dual[0, at]
            di = cat([ei + ti, ei - ti], 0) - dual[1, at]
            base[0, at] = -dr
            base[1, at] = -di
            pr, pi = probe[0], probe[1]
            add_window(acc, 0, top, left, pr * dr + pi * di)
            add_window(acc, 1, top, left, pr * di - pi * dr)

    def pair(index, carry):
        many([2 * index, 2 * index + 1])
        return carry

    lax.fori_loop(live, slots, skip, 0)

    @pl.when(live == 4)
    def _():
        many([0, 1, 2, 3])

    @pl.when((live == 2) | (live == 3))
    def _():
        many([0, 1])

    @pl.when(live % 2 == 1)
    def _():
        many([live - 1])


def dual_kernel(tile, half, offsets, live, ext, probe, base, out, new, ready, sems):
    slots = base.shape[1]
    size = 2 * half
    keep = pltpu.make_async_copy(ext.at[:, half : half + tile, half : half + tile], new, sems.at[slots])
    keep.start()
    copies = []
    for slot in range(slots):
        copy = pltpu.make_async_copy(ready.at[slot], out.at[:, slot], sems.at[slot])
        copies.append(copy)
        active = slot < live[0, 0]

        @pl.when(jnp.logical_not(active))
        def _():
            ready[slot] = base[:, slot]

        @pl.when(active)
        def _():
            top = offsets[0, 0, 0, slot]
            left = offsets[1, 0, 0, slot]
            pr, pi = probe[0], probe[1]
            sr = load_window(ext, 0, top, left, size)
            si = load_window(ext, 1, top, left, size)
            ready[slot, 0] = base[0, slot] + (pr * sr - pi * si)
            ready[slot, 1] = base[1, slot] + (pr * si + pi * sr)

        copy.start()
    for copy in copies:
        copy.wait()
    keep.wait()


def shards(object_field, probe, dual, amplitude, offsets, live):
    tile = object_field.shape[1]
    size = probe.shape[1]
    half = size // 2
    slots = dual.shape[3]
    wide = tile + size
    mid = tile - size
    amps = amplitude.reshape(slots, size, size)
    sd = lambda *shape: jax.ShapeDtypeStruct(shape, F32)
    dma = lambda n: pltpu.SemaphoreType.DMA((n,))
    wt, tw = tables(size)
    fixed = lambda x: pltpu.with_memory_space_constraint(x, pltpu.HBM)

    frame, lam, wt, probe, weight, acc, amps = pl.pallas_call(
        functools.partial(halo_kernel, tile, half),
        out_shape=(
            sd(2, wide, wide),
            sd(2, slots, size, size),
            jax.ShapeDtypeStruct(wt.shape, wt.dtype),
            sd(2, size, size),
            sd(tile, tile),
            sd(2, wide, wide),
            sd(slots, 2 * size, half),
        ),
        in_specs=[HBM, SM, HBM, HBM, HBM, HBM, HBM],
        out_specs=(VM,) * 7,
        scratch_shapes=[
            pltpu.SMEM(offsets.shape, jnp.int32),
            pltpu.VMEM((3, 3, ROWS, LANES), jnp.int32),
            pltpu.VMEM((ROWS, LANES), jnp.int32),
            pltpu.VMEM((slots, size, size), F32),
            pltpu.VMEM((size // LANES, size, LANES), F32),
            pltpu.VMEM((2, mid // 2, half), F32),
            pltpu.VMEM((2, mid // 2, half), F32),
            pltpu.VMEM((2, half, half), F32),
            dma(40),
            dma(40),
            dma(6),
        ],
        compiler_params=pltpu.CompilerParams(collective_id=0, has_side_effects=True, vmem_limit_bytes=16 * MIB),
        cost_estimate=pl.CostEstimate(flops=0, bytes_accessed=80_000_000, transcendentals=0),
        name="halo",
    )(fixed(offsets), live, fixed(object_field), fixed(dual.reshape(2, slots, size, size)), fixed(wt), fixed(probe), fixed(amps))

    cost = lambda size: pl.CostEstimate(flops=0, bytes_accessed=size, transcendentals=0)
    base, acc = pl.pallas_call(
        functools.partial(project_kernel, tile, half),
        out_shape=(sd(2, slots, size, size), sd(2, wide, wide)),
        in_specs=[SM, SM] + [VM] * 7,
        out_specs=(VM, VM),
        input_output_aliases={8: 1},
        compiler_params=pltpu.CompilerParams(vmem_limit_bytes=20 * MIB),
        cost_estimate=cost(30_000_000),
        name="project",
    )(offsets, live, lam, frame, probe, amps, wt, tw, acc)

    strip, side, end, via = (2, half, wide), (2, mid, half), (2, 2, half, half), (3, 2, max(half, mid // 2), half)
    frame = pl.pallas_call(
        functools.partial(update_kernel, tile, half),
        out_shape=sd(2, wide, wide),
        in_specs=[VM] * 3,
        out_specs=VM,
        scratch_shapes=[pltpu.VMEM(x, F32) for x in (strip, strip, side, side, end, end, end, end, via, via)] + [dma(60), dma(60)],
        compiler_params=pltpu.CompilerParams(collective_id=1, has_side_effects=True, vmem_limit_bytes=8 * MIB),
        cost_estimate=cost(150_000_000),
        name="update",
    )(acc, object_field, weight)

    dual_new, new = pl.pallas_call(
        functools.partial(dual_kernel, tile, half),
        out_shape=(sd(2, slots, size, size), sd(2, tile, tile)),
        in_specs=[SM, SM, VM, VM, VM],
        out_specs=(ANY, ANY),
        scratch_shapes=[pltpu.VMEM((slots, 2, size, size), F32), dma(slots + 1)],
        compiler_params=pltpu.CompilerParams(vmem_limit_bytes=12 * MIB),
        name="renew",
    )(offsets, live, frame, probe, base)
    return new, dual_new.reshape(dual.shape)


def solution(mesh):
    placed = (
        P(None, "row", "col"),
        P(),
        P(None, "row", "col", None, None, None),
        P("row", "col", None, None, None),
        P(None, "row", "col", None),
        P("row", "col"),
    )
    return jax.shard_map(
        shards,
        mesh=mesh,
        in_specs=placed,
        out_specs=(P(None, "row", "col"), P(None, "row", "col", None, None, None)),
        check_vma=False,
    )
```

```python
import functools
import math

import jax
import jax.numpy as jnp
import numpy as np
from jax import lax
from jax.experimental import pallas as pl
from jax.experimental.pallas import tpu as pltpu
from jax.sharding import PartitionSpec as P

FLOOR = 0.1
BETA = 1.0
LANES = 128
ROWS = 8
MIB = 1 << 20
F32 = jnp.float32
BF16 = jnp.bfloat16
ANY = pl.BlockSpec(memory_space=pl.ANY)
VM = pl.BlockSpec(memory_space=pltpu.VMEM)
SM = pl.BlockSpec(memory_space=pltpu.SMEM)
HBM = pl.BlockSpec(memory_space=pltpu.HBM)


def tables(size):
    n = size // 2
    k = np.arange(n)
    angle = 2.0 * math.pi * ((k[:, None] * k[None, :]) % n) / n
    c, s = np.cos(angle) / math.sqrt(size), np.sin(angle) / math.sqrt(size)
    fwd = np.block([[c, s], [-s, c]])
    inv = np.block([[c, -s], [s, c]])
    angle = angle + 2.0 * math.pi * k[None, :] / size
    c, s = np.cos(angle) / math.sqrt(size), np.sin(angle) / math.sqrt(size)
    odd = np.block([[c, s], [-s, c]])
    parts = []
    for full in (fwd, inv, odd, odd.T):
        hi = full.astype(np.float32).astype(BF16)
        parts += [hi, (full - hi.astype(np.float64)).astype(np.float32).astype(BF16)]
    perm = np.zeros((size, size), np.float32)
    perm[2 * k, k] = 1.0
    perm[2 * k + 1, n + k] = 1.0
    return jnp.asarray(np.stack(parts + [perm.astype(BF16)]))


def split(x):
    hi = x.astype(BF16)
    return hi, (x - hi.astype(F32)).astype(BF16)


def dot(a, b):
    return jnp.dot(a, b, preferred_element_type=F32)


def left_dot(wh, wl, x):
    xh, xl = split(x)
    return dot(wl, xh) + dot(wh, xl) + dot(wh, xh)


def right_dot(x, wh, wl):
    xh, xl = split(x)
    return dot(xh, wl) + dot(xl, wh) + dot(xh, wh)


def cat(parts, axis):
    return jnp.concatenate(parts, axis=axis)


def load_window(ext, channel, top, left, size):
    row = pl.multiple_of((top // ROWS) * ROWS, ROWS)
    base = pl.multiple_of((left // LANES) * LANES, LANES)
    width, height = size + LANES, size + ROWS
    wide = ext[channel, pl.ds(row, height), pl.ds(base, width)]
    wide = pltpu.roll(wide, (width - (left - base)) % width, 1)[:, :size]
    return pltpu.roll(wide, (height - (top - row)) % height, 0)[:size]


def add_window(acc, channel, top, left, value):
    size = value.shape[0]
    row = pl.multiple_of((top // ROWS) * ROWS, ROWS)
    base = pl.multiple_of((left // LANES) * LANES, LANES)
    width, height = size + LANES, size + ROWS
    wide = cat([value, jnp.zeros((ROWS, size), F32)], 0)
    wide = pltpu.roll(wide, top - row, 0)
    wide = cat([wide, jnp.zeros((height, LANES), F32)], 1)
    wide = pltpu.roll(wide, left - base, 1)
    acc[channel, pl.ds(row, height), pl.ds(base, width)] += wide


def clear_beyond(grid, tile, half, frame):
    end = half + tile
    strips = (
        ("up", slice(0, half), slice(None)),
        ("down", slice(end, None), slice(None)),
        ("left", slice(half, end), slice(0, half)),
        ("right", slice(half, end), slice(end, None)),
    )
    for side, rows, cols in strips:

        @pl.when(jnp.logical_not(grid.has[side]))
        def _():
            frame[:, rows, cols] = jnp.zeros_like(frame[:, rows, cols])

    for up, rows in (("up", slice(0, half)), ("down", slice(end, None))):
        for side, cols in (("left", slice(0, half)), ("right", slice(end, None))):

            @pl.when(grid.has[up] & jnp.logical_not(grid.has[side]))
            def _():
                frame[:, rows, cols] = jnp.zeros_like(frame[:, rows, cols])


CHUNKS = 4


class Grid:
    def __init__(self, send, recv):
        row, col = lax.axis_index("row"), lax.axis_index("col")
        self.col, self.cols = col, lax.axis_size("col")
        self.has = {
            "up": row > 0,
            "down": row < lax.axis_size("row") - 1,
            "left": col > 0,
            "right": col < self.cols - 1,
        }
        self.peer = {"up": {"row": row - 1}, "down": {"row": row + 1}, "left": {"col": col - 1}, "right": {"col": col + 1}}
        self.back = {"up": "down", "down": "up", "left": "right", "right": "left"}
        self.step = {"left": -1, "right": 1}
        self.send, self.recv = send, recv
        self.count = 0

    def bends(self):
        return self.cols % 2 == 0 and self.cols > 2

    def relayed(self, col, side, rank):
        gaps = self.cols // 2 - 1
        if side == "right":
            share = CHUNKS * (gaps - col // 2) // (gaps + 1)
            return (col % 2 == 1) & (col > 0) & (col < self.cols - 1) & (rank < share)
        share = CHUNKS * (col // 2) // (gaps + 1)
        return (col % 2 == 0) & (col > 0) & (col < self.cols) & (rank < share)

    def greet(self, between=None):
        barrier = pltpu.get_barrier_semaphore()
        col = self.col
        signals = [(self.has[side], self.peer[side]) for side in self.has]
        waits = sum(h.astype(jnp.int32) for h in self.has.values())
        if self.bends():
            signals.append((self.relayed(col - 1, "right", 0), {"col": col - 2}))
            signals.append((self.relayed(col + 1, "left", 0), {"col": col + 2}))
            waits += self.relayed(col + 1, "right", 0).astype(jnp.int32)
            waits += self.relayed(col - 1, "left", 0).astype(jnp.int32)
        for goes, peer in signals:

            @pl.when(goes)
            def _():
                pl.semaphore_signal(barrier, inc=1, device_id=peer, device_id_type=pl.DeviceIdType.MESH)

        if between is not None:
            between()
        pl.semaphore_wait(barrier, waits)

    def copy(self, peer, src, dst):
        at = self.count
        self.count += 1
        return pltpu.make_async_remote_copy(
            src_ref=src,
            dst_ref=dst,
            send_sem=self.send.at[at],
            recv_sem=self.recv.at[at],
            device_id=peer,
            device_id_type=pl.DeviceIdType.MESH,
        )

    def message(self, side, src, dst, also=None):
        goes, comes = self.has[side], self.has[self.back[side]]
        if also is not None:
            goes, comes = goes & self.has[also], comes & self.has[also]
        return self.copy(self.peer[side], src, dst), goes, comes

    def strip(self, side, rank, src, dst, relay):
        return Strip(self, side, rank, src, dst, relay)


class Strip:
    def __init__(self, grid, side, rank, src, dst, relay):
        step, col = grid.step[side], grid.col
        goes, comes = grid.has[side], grid.has[grid.back[side]]
        self.hops = []
        if grid.bends() and relay is not None:
            first, then, last = (grid.relayed(col + step * at, side, rank) for at in (0, 1, -1))
            goes, comes = goes & jnp.logical_not(first), comes & jnp.logical_not(last)
            self.hops.append((grid.copy({"col": col - step}, src, relay), first, then))
            self.hops.append((grid.copy({"col": col + 2 * step}, relay, dst), then, last))
        self.direct = grid.copy(grid.peer[side], src, dst), goes, comes

    def begin(self):
        start(*self.hops[:1])

    def begun(self):
        leave(*self.hops[:1])

    def rest(self):
        start(self.direct)

    def start(self):
        self.begin()
        self.rest()

    def forward(self):
        if self.hops:
            (first, _, comes), (then, _, _) = self.hops

            @pl.when(comes)
            def _():
                first.wait_recv()
                then.start()

    def arrive(self):
        arrive(*self.hops[1:], self.direct)

    def leave(self):
        leave(*self.hops[1:], self.direct)


def when(cond, act):
    if cond is True:
        act()
    else:
        pl.when(cond)(act)


def start(*messages):
    for m in messages:
        if isinstance(m, Strip):
            m.start()
        else:
            pl.when(m[1])(m[0].start)


def each(act, *strips):
    for m in strips:
        getattr(m, act)()


def forward(*strips):
    each("forward", *strips)


def arrive(*messages):
    for m in messages:
        if isinstance(m, Strip):
            m.arrive()
        else:
            pl.when(m[2])(m[0].wait_recv)


def leave(*messages):
    for m in messages:
        if isinstance(m, Strip):
            m.leave()
        else:
            pl.when(m[1])(m[0].wait_send)


def column_messages(grid, tile, half, src, frame, relay):
    size, end = 2 * half, half + tile
    mid = (tile - size) // 2
    rows = [slice(half, half + mid), slice(half + mid, tile - half), slice(0, half), slice(tile - half, tile)]
    groups = []
    for rank, at in enumerate(rows):
        store = slice(at.start + half, at.stop + half)
        via = relay[rank] if rank < len(relay) else None
        groups.append(
            [
                grid.strip("left", rank, src.at[:, at, :half], frame.at[:, store, end:], via),
                grid.strip("right", rank, src.at[:, at, tile - half :], frame.at[:, store, :half], via),
            ]
        )
    return groups[2] + groups[3], groups[0] + groups[1]


def row_messages(grid, tile, half, src, frame):
    end = half + tile
    return [
        grid.message("up", src.at[:, :half, :], frame.at[:, end:, half:end]),
        grid.message("down", src.at[:, tile - half :, :], frame.at[:, :half, half:end]),
    ]


def corner_messages(grid, tile, half, frame):
    size, end = 2 * half, half + tile
    out = []
    for side, cols in (("left", slice(0, half)), ("right", slice(end, None))):
        out.append(grid.message("up", frame.at[:, half:size, cols], frame.at[:, end:, cols], also=side))
        out.append(grid.message("down", frame.at[:, tile:end, cols], frame.at[:, :half, cols], also=side))
    return out


def one_hot(shape, shift):
    gap = lax.broadcasted_iota(jnp.int32, shape, 0) - lax.broadcasted_iota(jnp.int32, shape, 1)
    return jnp.where(gap == shift, 1.0, 0.0).astype(BF16)


def spread_power(tile, half, slots, bands, infos, probe, weight):
    size = 2 * half
    high, low = split(probe[0] * probe[0] + probe[1] * probe[1])
    spans = [
        (slice(0, half), slice(half, size), -tile),
        (slice(0, tile), slice(0, size), 0),
        (slice(tile - half, tile), slice(0, half), tile),
    ]
    for r in bands:
        rows, along, row_at = spans[r]
        for c, (cols, across, col_at) in enumerate(spans):
            ny, nk = rows.stop - rows.start, along.stop - along.start
            nx, nl = cols.stop - cols.start, across.stop - across.start
            part = cat([high[along, across], low[along, across]], 0)
            total = weight[rows, cols]
            for slot in range(slots):
                used = slot < infos[r, c, :1, 2 * slots : 2 * slots + 1]
                top = infos[r, c, :1, slot : slot + 1] + (row_at - half - rows.start + along.start)
                left = infos[r, c, :1, slots + slot : slots + slot + 1] + (col_at - half - cols.start + across.start)
                top = jnp.where(used, top, 2 * tile)
                moved = dot(part, one_hot((nl, nx), -left)).astype(BF16)
                place = one_hot((ny, nk), top)
                total = total + dot(place, moved[:nk]) + dot(place, moved[nk:])
            weight[rows, cols] = total


def sort_amplitude(slots, amp, strips, perm, out):
    count, size = strips.shape[0], strips.shape[1]
    half = size // 2
    for slot in range(slots):
        for c in range(count):
            strips[c] = amp[slot, :, c * LANES : (c + 1) * LANES]
        rows = []
        for first in range(2):
            rows.append(cat([strips[c, pl.ds(first, half, stride=2), :] for c in range(count)], 1))
        high, low = split(cat(rows, 0))
        a = dot(high, perm) + dot(low, perm)
        out[slot] = cat([a[:, :half], a[:, half:]], 0)


def halo_kernel(tile, half, places, live, cells, dual, wt, probe, amp, *refs):
    frame, lam, tables_out, probe_out, weight, acc, sorted_amp = refs[:7]
    offsets, infos, tag, plain_amp, strips, r0, r1, r2, send, recv, local = refs[7:]
    grid = Grid(send, recv)
    has = grid.has
    slots = offsets.shape[3]
    scalars = pltpu.make_async_copy(places, offsets, local.at[5])
    scalars.start()
    loads = [
        pltpu.make_async_copy(probe, probe_out, local.at[0]),
        pltpu.make_async_copy(cells, frame.at[:, half : half + tile, half : half + tile], local.at[1]),
        pltpu.make_async_copy(dual, lam, local.at[2]),
        pltpu.make_async_copy(wt, tables_out, local.at[3]),
        pltpu.make_async_copy(amp, plain_amp, local.at[4]),
    ]
    ends, inner = column_messages(grid, tile, half, cells, frame, (r0, r1, r2))
    rows = row_messages(grid, tile, half, cells, frame)
    corners = corner_messages(grid, tile, half, frame)
    tags = [
        grid.message("left", tag, infos.at[1, 2]),
        grid.message("right", tag, infos.at[1, 0]),
    ]
    bands = [
        grid.message("up", infos.at[1], infos.at[2]),
        grid.message("down", infos.at[1], infos.at[0]),
    ]

    def make_tag():
        scalars.wait()
        lane = lax.broadcasted_iota(jnp.int32, tag.shape, 1)
        value = jnp.where(lane == 2 * slots, live[0, 0], 0)
        for k in range(slots):
            value = jnp.where(lane == k, offsets[0, 0, 0, k], value)
            value = jnp.where(lane == slots + k, offsets[1, 0, 0, k], value)
        tag[...] = value
        infos[1, 1] = value

    grid.greet(make_tag)
    start(*tags)
    each("begin", *inner, *ends)
    each("rest", *ends)
    for copy in loads:
        copy.start()
    clear_beyond(grid, tile, half, frame)
    for side, at in (("left", (1, 0)), ("right", (1, 2)), ("up", (0,)), ("down", (2,))):

        @pl.when(jnp.logical_not(has[side]))
        def _():
            infos[at] = jnp.zeros_like(infos[at])

    arrive(*tags)
    start(*bands, *rows)
    each("begun", *inner, *ends)
    each("rest", *inner)
    forward(*inner, *ends)
    loads[0].wait()
    arrive(*bands)
    acc[...] = jnp.zeros_like(acc)
    weight[...] = jnp.full_like(weight, BETA)
    spread_power(tile, half, slots, (0, 2), infos, probe_out, weight)
    arrive(*ends)
    start(*corners)
    spread_power(tile, half, slots, (1,), infos, probe_out, weight)
    for copy in loads[1:]:
        copy.wait()
    sort_amplitude(slots, plain_amp, strips, tables_out[8], sorted_amp)
    arrive(*inner, *rows, *corners)
    leave(*tags, *ends, *inner, *rows, *bands, *corners)


def update_kernel(tile, half, *refs):
    acc, cells, weight, frame = refs[:4]
    fa, fb, g_lm, g_rm, g_le, g_re, s_le, s_re, sums, news, send, recv = refs[4:]
    size, end = 2 * half, half + tile
    grid = Grid(send, recv)
    has = grid.has
    val = frame.at[:, half:end, half:end]
    up = grid.message("up", acc.at[:, :half, :], fb)
    down = grid.message("down", acc.at[:, end:, :], fa)
    mid = (tile - size) // 2
    mids = []
    for rank in range(2):
        at, to = slice(size + rank * mid, size + (rank + 1) * mid), slice(rank * mid, (rank + 1) * mid)
        mids.append(grid.strip("left", rank, acc.at[:, at, :half], g_rm.at[:, to], sums.at[rank, :, :mid]))
        mids.append(grid.strip("right", rank, acc.at[:, at, end:], g_lm.at[:, to], sums.at[rank, :, :mid]))
    ends = []
    for at in range(2):
        via = sums.at[2] if at == 0 else None
        ends.append(grid.strip("left", 2 + at, s_le.at[:, at], g_re.at[:, at], via))
        ends.append(grid.strip("right", 2 + at, s_re.at[:, at], g_le.at[:, at], via))
    via = [news.at[0, :, :mid], news.at[1, :, :mid], news.at[2]]
    new_ends, new_inner = column_messages(grid, tile, half, val, frame, via)
    new_rows = row_messages(grid, tile, half, val, frame)
    corners = corner_messages(grid, tile, half, frame)
    grid.greet()
    each("begin", *mids)
    start(up, down)
    each("rest", *mids)
    clear_beyond(grid, tile, half, frame)
    for side, buffers in (("up", (fa,)), ("down", (fb,)), ("left", (g_lm, g_le)), ("right", (g_rm, g_re))):

        @pl.when(jnp.logical_not(has[side]))
        def _():
            for b in buffers:
                b[...] = jnp.zeros_like(b)

    arrive(up, down)
    for ch in range(2):
        s_le[ch, 0] = acc[ch, half:size, :half] + fa[ch, :, :half]
        s_le[ch, 1] = acc[ch, tile:end, :half] + fb[ch, :, :half]
        s_re[ch, 0] = acc[ch, half:size, end:] + fa[ch, :, end:]
        s_re[ch, 1] = acc[ch, tile:end, end:] + fb[ch, :, end:]
    start(*ends)
    tops, bottoms, inner = slice(0, half), slice(tile - half, tile), slice(half, tile - half)
    heads, tails = slice(0, half), slice(tile - half, tile)

    def moved(at):
        return slice(at.start + half, at.stop + half)

    def settle(ch, rows, cols, more):
        total = acc[ch, moved(rows), moved(cols)] + BETA * cells[ch, rows, cols]
        for m in more:
            total = total + m
        frame[ch, moved(rows), moved(cols)] = total / weight[rows, cols]

    forward(*mids)
    for ch in range(2):
        settle(ch, inner, inner, ())
        settle(ch, tops, inner, (fa[ch, :, size:tile],))
        settle(ch, bottoms, inner, (fb[ch, :, size:tile],))
    arrive(*mids)
    for ch in range(2):
        settle(ch, inner, heads, (g_lm[ch],))
        settle(ch, inner, tails, (g_rm[ch],))
    first, second = [], new_inner
    forward(*ends)
    arrive(*ends)
    for ch in range(2):
        settle(ch, tops, heads, (fa[ch, :, half:size], g_le[ch, 0]))
        settle(ch, bottoms, heads, (fb[ch, :, half:size], g_le[ch, 1]))
        settle(ch, tops, tails, (fa[ch, :, tile:end], g_re[ch, 0]))
        settle(ch, bottoms, tails, (fb[ch, :, tile:end], g_re[ch, 1]))
    each("begin", *new_ends, *second)
    each("rest", *new_ends)
    start(*new_rows)
    forward(*first)
    each("begun", *new_ends, *second)
    each("rest", *second)
    forward(*new_ends, *second)
    arrive(*new_ends)
    start(*corners)
    arrive(*new_inner, *new_rows, *corners)
    each("begun", *mids, *ends, *first)
    leave(up, down, *mids, *ends, *new_ends, *new_inner, *new_rows, *corners)


def project_kernel(tile, half, offsets, count, *refs):
    dual, ext, probe, amp, wt = refs[:5]
    base, acc = refs[6:]
    slots = dual.shape[1]
    size = 2 * half
    live = count[0, 0]

    def skip(slot, carry):
        base[:, slot] = dual[:, slot]
        return carry

    def many(slots_at):
        tops = [offsets[0, 0, 0, at] for at in slots_at]
        lefts = [offsets[1, 0, 0, at] for at in slots_at]
        fwd, inv, fwd_odd, inv_odd = ((wt[2 * at], wt[2 * at + 1]) for at in range(4))
        n = range(len(slots_at))
        x = []
        for at, top, left in zip(slots_at, tops, lefts):
            pr, pi = probe[0], probe[1]
            wr = load_window(ext, 0, top, left, size)
            wi = load_window(ext, 1, top, left, size)
            re = pr * wr - pi * wi + dual[0, at]
            im = pr * wi + pi * wr + dual[1, at]
            x.append(cat([re[:half] + re[half:], im[:half] + im[half:]], 0))
            x.append(cat([re[:half] - re[half:], im[:half] - im[half:]], 0))
        y = [left_dot(*(fwd_odd if at % 2 else fwd), v) for at, v in enumerate(x)]
        x = []
        for i in n:
            even, odd = y[2 * i], y[2 * i + 1]
            re = cat([even[:half], odd[:half]], 0)
            im = cat([even[half:], odd[half:]], 0)
            x.append(cat([re[:, :half] + re[:, half:], im[:, :half] + im[:, half:]], 1))
            x.append(cat([re[:, :half] - re[:, half:], im[:, :half] - im[:, half:]], 1))
        y = [right_dot(v, *(inv_odd if at % 2 else inv)) for at, v in enumerate(x)]
        x = []
        for i, at in enumerate(slots_at):
            for odd in range(2):
                b = amp[at, odd * size : (odd + 1) * size]
                v = y[2 * i + odd]
                re, im = v[:, :half], v[:, half:]
                fac = b * lax.rsqrt(jnp.maximum(re * re + im * im, FLOOR * FLOOR))
                x.append(cat([re * fac, im * fac], 1))
        y = [right_dot(v, *(fwd_odd if at % 2 else fwd)) for at, v in enumerate(x)]
        x = []
        for i in n:
            even, odd = y[2 * i], y[2 * i + 1]
            re = cat([even[:, :half] + odd[:, :half], even[:, :half] - odd[:, :half]], 1)
            im = cat([even[:, half:] + odd[:, half:], even[:, half:] - odd[:, half:]], 1)
            x.append(cat([re[:half], im[:half]], 0))
            x.append(cat([re[half:], im[half:]], 0))
        y = [left_dot(*(inv_odd if at % 2 else inv), v) for at, v in enumerate(x)]
        for i, (at, top, left) in enumerate(zip(slots_at, tops, lefts)):
            even, odd = y[2 * i], y[2 * i + 1]
            dr = cat([even[:half] + odd[:half], even[:half] - odd[:half]], 0) - dual[0, at]
            di = cat([even[half:] + odd[half:], even[half:] - odd[half:]], 0) - dual[1, at]
            base[0, at] = -dr
            base[1, at] = -di
            pr, pi = probe[0], probe[1]
            add_window(acc, 0, top, left, pr * dr + pi * di)
            add_window(acc, 1, top, left, pr * di - pi * dr)

    def pair(index, carry):
        many([2 * index, 2 * index + 1])
        return carry

    lax.fori_loop(live, slots, skip, 0)

    @pl.when(live == 4)
    def _():
        many([0, 1, 2, 3])

    @pl.when((live == 2) | (live == 3))
    def _():
        many([0, 1])

    @pl.when(live % 2 == 1)
    def _():
        many([live - 1])


def dual_kernel(tile, half, offsets, live, ext, probe, base, out, new, ready, sems):
    slots = base.shape[1]
    size = 2 * half
    keep = pltpu.make_async_copy(ext.at[:, half : half + tile, half : half + tile], new, sems.at[slots])
    keep.start()
    copies = []
    for slot in range(slots):
        copy = pltpu.make_async_copy(ready.at[slot], out.at[:, slot], sems.at[slot])
        copies.append(copy)
        active = slot < live[0, 0]

        @pl.when(jnp.logical_not(active))
        def _():
            ready[slot] = base[:, slot]

        @pl.when(active)
        def _():
            top = offsets[0, 0, 0, slot]
            left = offsets[1, 0, 0, slot]
            pr, pi = probe[0], probe[1]
            sr = load_window(ext, 0, top, left, size)
            si = load_window(ext, 1, top, left, size)
            ready[slot, 0] = base[0, slot] + (pr * sr - pi * si)
            ready[slot, 1] = base[1, slot] + (pr * si + pi * sr)

        copy.start()
    for copy in copies:
        copy.wait()
    keep.wait()


def shards(object_field, probe, dual, amplitude, offsets, live):
    tile = object_field.shape[1]
    size = probe.shape[1]
    half = size // 2
    slots = dual.shape[3]
    wide = tile + size
    mid = tile - size
    amps = amplitude.reshape(slots, size, size)
    sd = lambda *shape: jax.ShapeDtypeStruct(shape, F32)
    dma = lambda n: pltpu.SemaphoreType.DMA((n,))
    wt = tables(size)
    fixed = lambda x: pltpu.with_memory_space_constraint(x, pltpu.HBM)

    frame, lam, wt, probe, weight, acc, amps = pl.pallas_call(
        functools.partial(halo_kernel, tile, half),
        out_shape=(
            sd(2, wide, wide),
            sd(2, slots, size, size),
            jax.ShapeDtypeStruct(wt.shape, wt.dtype),
            sd(2, size, size),
            sd(tile, tile),
            sd(2, wide, wide),
            sd(slots, 2 * size, half),
        ),
        in_specs=[HBM, SM, HBM, HBM, HBM, HBM, HBM],
        out_specs=(VM,) * 7,
        scratch_shapes=[
            pltpu.SMEM(offsets.shape, jnp.int32),
            pltpu.VMEM((3, 3, ROWS, LANES), jnp.int32),
            pltpu.VMEM((ROWS, LANES), jnp.int32),
            pltpu.VMEM((slots, size, size), F32),
            pltpu.VMEM((size // LANES, size, LANES), F32),
            pltpu.VMEM((2, mid // 2, half), F32),
            pltpu.VMEM((2, mid // 2, half), F32),
            pltpu.VMEM((2, half, half), F32),
            dma(40),
            dma(40),
            dma(6),
        ],
        compiler_params=pltpu.CompilerParams(collective_id=0, has_side_effects=True, vmem_limit_bytes=16 * MIB),
        cost_estimate=pl.CostEstimate(flops=0, bytes_accessed=80_000_000, transcendentals=0),
        name="halo",
    )(fixed(offsets), live, fixed(object_field), fixed(dual.reshape(2, slots, size, size)), fixed(wt), fixed(probe), fixed(amps))

    cost = lambda size: pl.CostEstimate(flops=0, bytes_accessed=size, transcendentals=0)
    base, acc = pl.pallas_call(
        functools.partial(project_kernel, tile, half),
        out_shape=(sd(2, slots, size, size), sd(2, wide, wide)),
        in_specs=[SM, SM] + [VM] * 6,
        out_specs=(VM, VM),
        input_output_aliases={7: 1},
        compiler_params=pltpu.CompilerParams(vmem_limit_bytes=20 * MIB),
        cost_estimate=cost(30_000_000),
        name="project",
    )(offsets, live, lam, frame, probe, amps, wt, acc)

    strip, side, end, via = (2, half, wide), (2, mid, half), (2, 2, half, half), (3, 2, max(half, mid // 2), half)
    frame = pl.pallas_call(
        functools.partial(update_kernel, tile, half),
        out_shape=sd(2, wide, wide),
        in_specs=[VM] * 3,
        out_specs=VM,
        scratch_shapes=[pltpu.VMEM(x, F32) for x in (strip, strip, side, side, end, end, end, end, via, via)] + [dma(60), dma(60)],
        compiler_params=pltpu.CompilerParams(collective_id=1, has_side_effects=True, vmem_limit_bytes=8 * MIB),
        cost_estimate=cost(150_000_000),
        name="update",
    )(acc, object_field, weight)

    dual_new, new = pl.pallas_call(
        functools.partial(dual_kernel, tile, half),
        out_shape=(sd(2, slots, size, size), sd(2, tile, tile)),
        in_specs=[SM, SM, VM, VM, VM],
        out_specs=(ANY, ANY),
        scratch_shapes=[pltpu.VMEM((slots, 2, size, size), F32), dma(slots + 1)],
        compiler_params=pltpu.CompilerParams(vmem_limit_bytes=12 * MIB),
        name="renew",
    )(offsets, live, frame, probe, base)
    return new, dual_new.reshape(dual.shape)


def solution(mesh):
    placed = (
        P(None, "row", "col"),
        P(),
        P(None, "row", "col", None, None, None),
        P("row", "col", None, None, None),
        P(None, "row", "col", None),
        P("row", "col"),
    )
    return jax.shard_map(
        shards,
        mesh=mesh,
        in_specs=placed,
        out_specs=(P(None, "row", "col"), P(None, "row", "col", None, None, None)),
        check_vma=False,
    )
```

```python
import functools
import math

import jax
import jax.numpy as jnp
import numpy as np
from jax import lax
from jax.experimental import pallas as pl
from jax.experimental.pallas import tpu as pltpu
from jax.sharding import PartitionSpec as P

FLOOR = 0.1
BETA = 1.0
LANES = 128
ROWS = 8
MIB = 1 << 20
F32 = jnp.float32
BF16 = jnp.bfloat16
ANY = pl.BlockSpec(memory_space=pl.ANY)
VM = pl.BlockSpec(memory_space=pltpu.VMEM)
SM = pl.BlockSpec(memory_space=pltpu.SMEM)
HBM = pl.BlockSpec(memory_space=pltpu.HBM)


def tables(size):
    n = size // 2
    k = np.arange(n)
    angle = 2.0 * math.pi * ((k[:, None] * k[None, :]) % n) / n
    c, s = np.cos(angle) / math.sqrt(size), np.sin(angle) / math.sqrt(size)
    fwd = np.block([[c, s], [-s, c]])
    inv = np.block([[c, -s], [s, c]])
    angle = angle + 2.0 * math.pi * k[None, :] / size
    c, s = np.cos(angle) / math.sqrt(size), np.sin(angle) / math.sqrt(size)
    odd = np.block([[c, s], [-s, c]])
    parts = []
    for full in (fwd, inv, odd, odd.T):
        hi = full.astype(np.float32).astype(BF16)
        parts += [hi, (full - hi.astype(np.float64)).astype(np.float32).astype(BF16)]
    perm = np.zeros((size, size), np.float32)
    perm[2 * k, k] = 1.0
    perm[2 * k + 1, n + k] = 1.0
    return jnp.asarray(np.stack(parts + [perm.astype(BF16)]))


def split(x):
    hi = x.astype(BF16)
    return hi, (x - hi.astype(F32)).astype(BF16)


def dot(a, b):
    return jnp.dot(a, b, preferred_element_type=F32)


def left_dot(wh, wl, x):
    xh, xl = split(x)
    return dot(wl, xh) + dot(wh, xl) + dot(wh, xh)


def right_dot(x, wh, wl):
    xh, xl = split(x)
    return dot(xh, wl) + dot(xl, wh) + dot(xh, wh)


def cat(parts, axis):
    return jnp.concatenate(parts, axis=axis)


def load_window(ext, channel, top, left, size):
    row = pl.multiple_of((top // ROWS) * ROWS, ROWS)
    base = pl.multiple_of((left // LANES) * LANES, LANES)
    width, height = size + LANES, size + ROWS
    wide = ext[channel, pl.ds(row, height), pl.ds(base, width)]
    wide = pltpu.roll(wide, (width - (left - base)) % width, 1)[:, :size]
    return pltpu.roll(wide, (height - (top - row)) % height, 0)[:size]


def add_window(acc, channel, top, left, value):
    size = value.shape[0]
    row = pl.multiple_of((top // ROWS) * ROWS, ROWS)
    base = pl.multiple_of((left // LANES) * LANES, LANES)
    width, height = size + LANES, size + ROWS
    wide = cat([value, jnp.zeros((ROWS, size), F32)], 0)
    wide = pltpu.roll(wide, top - row, 0)
    wide = cat([wide, jnp.zeros((height, LANES), F32)], 1)
    wide = pltpu.roll(wide, left - base, 1)
    acc[channel, pl.ds(row, height), pl.ds(base, width)] += wide


def clear_beyond(grid, tile, half, frame):
    end = half + tile
    strips = (
        ("up", slice(0, half), slice(None)),
        ("down", slice(end, None), slice(None)),
        ("left", slice(half, end), slice(0, half)),
        ("right", slice(half, end), slice(end, None)),
    )
    for side, rows, cols in strips:

        @pl.when(jnp.logical_not(grid.has[side]))
        def _():
            frame[:, rows, cols] = jnp.zeros_like(frame[:, rows, cols])

    for up, rows in (("up", slice(0, half)), ("down", slice(end, None))):
        for side, cols in (("left", slice(0, half)), ("right", slice(end, None))):

            @pl.when(grid.has[up] & jnp.logical_not(grid.has[side]))
            def _():
                frame[:, rows, cols] = jnp.zeros_like(frame[:, rows, cols])


CHUNKS = 4


class Grid:
    def __init__(self, send, recv):
        row, col = lax.axis_index("row"), lax.axis_index("col")
        self.col, self.cols = col, lax.axis_size("col")
        self.has = {
            "up": row > 0,
            "down": row < lax.axis_size("row") - 1,
            "left": col > 0,
            "right": col < self.cols - 1,
        }
        self.peer = {"up": {"row": row - 1}, "down": {"row": row + 1}, "left": {"col": col - 1}, "right": {"col": col + 1}}
        self.back = {"up": "down", "down": "up", "left": "right", "right": "left"}
        self.step = {"left": -1, "right": 1}
        self.send, self.recv = send, recv
        self.count = 0

    def bends(self):
        return self.cols % 2 == 0 and self.cols > 2

    def relayed(self, col, side, rank):
        gaps = self.cols // 2 - 1
        if side == "right":
            share = CHUNKS * (gaps - col // 2) // (gaps + 1)
            return (col % 2 == 1) & (col > 0) & (col < self.cols - 1) & (rank < share)
        share = CHUNKS * (col // 2) // (gaps + 1)
        return (col % 2 == 0) & (col > 0) & (col < self.cols) & (rank < share)

    def greet(self, between=None):
        barrier = pltpu.get_barrier_semaphore()
        col = self.col
        signals = [(self.has[side], self.peer[side]) for side in self.has]
        waits = sum(h.astype(jnp.int32) for h in self.has.values())
        if self.bends():
            signals.append((self.relayed(col - 1, "right", 0), {"col": col - 2}))
            signals.append((self.relayed(col + 1, "left", 0), {"col": col + 2}))
            waits += self.relayed(col + 1, "right", 0).astype(jnp.int32)
            waits += self.relayed(col - 1, "left", 0).astype(jnp.int32)
        for goes, peer in signals:

            @pl.when(goes)
            def _():
                pl.semaphore_signal(barrier, inc=1, device_id=peer, device_id_type=pl.DeviceIdType.MESH)

        if between is not None:
            between()
        pl.semaphore_wait(barrier, waits)

    def copy(self, peer, src, dst):
        at = self.count
        self.count += 1
        return pltpu.make_async_remote_copy(
            src_ref=src,
            dst_ref=dst,
            send_sem=self.send.at[at],
            recv_sem=self.recv.at[at],
            device_id=peer,
            device_id_type=pl.DeviceIdType.MESH,
        )

    def message(self, side, src, dst, also=None):
        goes, comes = self.has[side], self.has[self.back[side]]
        if also is not None:
            goes, comes = goes & self.has[also], comes & self.has[also]
        return self.copy(self.peer[side], src, dst), goes, comes

    def strip(self, side, rank, src, dst, relay):
        return Strip(self, side, rank, src, dst, relay)


class Strip:
    def __init__(self, grid, side, rank, src, dst, relay):
        step, col = grid.step[side], grid.col
        goes, comes = grid.has[side], grid.has[grid.back[side]]
        self.hops = []
        if grid.bends() and relay is not None:
            first, then, last = (grid.relayed(col + step * at, side, rank) for at in (0, 1, -1))
            goes, comes = goes & jnp.logical_not(first), comes & jnp.logical_not(last)
            self.hops.append((grid.copy({"col": col - step}, src, relay), first, then))
            self.hops.append((grid.copy({"col": col + 2 * step}, relay, dst), then, last))
        self.direct = grid.copy(grid.peer[side], src, dst), goes, comes

    def begin(self):
        start(*self.hops[:1])

    def begun(self):
        leave(*self.hops[:1])

    def rest(self):
        start(self.direct)

    def start(self):
        self.begin()
        self.rest()

    def forward(self):
        if self.hops:
            (first, _, comes), (then, _, _) = self.hops

            @pl.when(comes)
            def _():
                first.wait_recv()
                then.start()

    def arrive(self):
        arrive(*self.hops[1:], self.direct)

    def leave(self):
        leave(*self.hops[1:], self.direct)


def when(cond, act):
    if cond is True:
        act()
    else:
        pl.when(cond)(act)


def start(*messages):
    for m in messages:
        if isinstance(m, Strip):
            m.start()
        else:
            pl.when(m[1])(m[0].start)


def each(act, *strips):
    for m in strips:
        getattr(m, act)()


def forward(*strips):
    each("forward", *strips)


def arrive(*messages):
    for m in messages:
        if isinstance(m, Strip):
            m.arrive()
        else:
            pl.when(m[2])(m[0].wait_recv)


def leave(*messages):
    for m in messages:
        if isinstance(m, Strip):
            m.leave()
        else:
            pl.when(m[1])(m[0].wait_send)


def column_messages(grid, tile, half, src, frame, relay):
    size, end = 2 * half, half + tile
    mid = (tile - size) // 2
    rows = [slice(half, half + mid), slice(half + mid, tile - half), slice(0, half), slice(tile - half, tile)]
    groups = []
    for rank, at in enumerate(rows):
        store = slice(at.start + half, at.stop + half)
        via = relay[rank] if rank < len(relay) else None
        groups.append(
            [
                grid.strip("left", rank, src.at[:, at, :half], frame.at[:, store, end:], via),
                grid.strip("right", rank, src.at[:, at, tile - half :], frame.at[:, store, :half], via),
            ]
        )
    return groups[2] + groups[3], groups[0] + groups[1]


def row_messages(grid, tile, half, src, frame):
    end = half + tile
    return [
        grid.message("up", src.at[:, :half, :], frame.at[:, end:, half:end]),
        grid.message("down", src.at[:, tile - half :, :], frame.at[:, :half, half:end]),
    ]


def corner_messages(grid, tile, half, frame):
    size, end = 2 * half, half + tile
    out = []
    for side, cols in (("left", slice(0, half)), ("right", slice(end, None))):
        out.append(grid.message("up", frame.at[:, half:size, cols], frame.at[:, end:, cols], also=side))
        out.append(grid.message("down", frame.at[:, tile:end, cols], frame.at[:, :half, cols], also=side))
    return out


def one_hot(shape, shift):
    gap = lax.broadcasted_iota(jnp.int32, shape, 0) - lax.broadcasted_iota(jnp.int32, shape, 1)
    return jnp.where(gap == shift, 1.0, 0.0).astype(BF16)


def spread_power(tile, half, slots, bands, infos, probe, weight):
    size = 2 * half
    high, low = split(probe[0] * probe[0] + probe[1] * probe[1])
    spans = [
        (slice(0, half), slice(half, size), -tile),
        (slice(0, tile), slice(0, size), 0),
        (slice(tile - half, tile), slice(0, half), tile),
    ]
    for r in bands:
        rows, along, row_at = spans[r]
        for c, (cols, across, col_at) in enumerate(spans):
            ny, nk = rows.stop - rows.start, along.stop - along.start
            nx, nl = cols.stop - cols.start, across.stop - across.start
            part = cat([high[along, across], low[along, across]], 0)
            total = weight[rows, cols]
            for slot in range(slots):
                used = slot < infos[r, c, :1, 2 * slots : 2 * slots + 1]
                top = infos[r, c, :1, slot : slot + 1] + (row_at - half - rows.start + along.start)
                left = infos[r, c, :1, slots + slot : slots + slot + 1] + (col_at - half - cols.start + across.start)
                top = jnp.where(used, top, 2 * tile)
                moved = dot(part, one_hot((nl, nx), -left)).astype(BF16)
                place = one_hot((ny, nk), top)
                total = total + dot(place, moved[:nk]) + dot(place, moved[nk:])
            weight[rows, cols] = total


def sort_amplitude(slots, amp, strips, perm, out):
    count, size = strips.shape[0], strips.shape[1]
    half = size // 2
    for slot in range(slots):
        for c in range(count):
            strips[c] = amp[slot, :, c * LANES : (c + 1) * LANES]
        rows = []
        for first in range(2):
            rows.append(cat([strips[c, pl.ds(first, half, stride=2), :] for c in range(count)], 1))
        high, low = split(cat(rows, 0))
        a = dot(high, perm) + dot(low, perm)
        out[slot] = cat([a[:, :half], a[:, half:]], 0)


def halo_kernel(tile, half, places, live, cells, dual, wt, probe, amp, *refs):
    frame, lam, tables_out, probe_out, weight, acc, sorted_amp = refs[:7]
    offsets, infos, tag, plain_amp, strips, r0, r1, r2, send, recv, local = refs[7:]
    grid = Grid(send, recv)
    has = grid.has
    slots = offsets.shape[3]
    scalars = pltpu.make_async_copy(places, offsets, local.at[5])
    scalars.start()
    loads = [
        pltpu.make_async_copy(probe, probe_out, local.at[0]),
        pltpu.make_async_copy(cells, frame.at[:, half : half + tile, half : half + tile], local.at[1]),
        pltpu.make_async_copy(dual, lam, local.at[2]),
        pltpu.make_async_copy(wt, tables_out, local.at[3]),
        pltpu.make_async_copy(amp, plain_amp, local.at[4]),
    ]
    ends, inner = column_messages(grid, tile, half, cells, frame, (r0, r1, r2))
    rows = row_messages(grid, tile, half, cells, frame)
    corners = corner_messages(grid, tile, half, frame)
    tags = [
        grid.message("left", tag, infos.at[1, 2]),
        grid.message("right", tag, infos.at[1, 0]),
    ]
    bands = [
        grid.message("up", infos.at[1], infos.at[2]),
        grid.message("down", infos.at[1], infos.at[0]),
    ]

    def make_tag():
        scalars.wait()
        lane = lax.broadcasted_iota(jnp.int32, tag.shape, 1)
        value = jnp.where(lane == 2 * slots, live[0, 0], 0)
        for k in range(slots):
            value = jnp.where(lane == k, offsets[0, 0, 0, k], value)
            value = jnp.where(lane == slots + k, offsets[1, 0, 0, k], value)
        tag[...] = value
        infos[1, 1] = value

    grid.greet(make_tag)
    start(*tags)
    each("begin", *inner, *ends)
    each("rest", *ends)
    for copy in loads:
        copy.start()
    clear_beyond(grid, tile, half, frame)
    for side, at in (("left", (1, 0)), ("right", (1, 2)), ("up", (0,)), ("down", (2,))):

        @pl.when(jnp.logical_not(has[side]))
        def _():
            infos[at] = jnp.zeros_like(infos[at])

    arrive(*tags)
    start(*bands, *rows)
    each("begun", *inner, *ends)
    each("rest", *inner)
    forward(*inner, *ends)
    loads[0].wait()
    arrive(*bands)
    acc[...] = jnp.zeros_like(acc)
    weight[...] = jnp.full_like(weight, BETA)
    spread_power(tile, half, slots, (0, 2), infos, probe_out, weight)
    arrive(*ends)
    start(*corners)
    spread_power(tile, half, slots, (1,), infos, probe_out, weight)
    for copy in loads[1:]:
        copy.wait()
    sort_amplitude(slots, plain_amp, strips, tables_out[8], sorted_amp)
    arrive(*inner, *rows, *corners)
    leave(*tags, *ends, *inner, *rows, *bands, *corners)


def update_kernel(tile, half, *refs):
    acc, cells, weight, frame = refs[:4]
    fa, fb, g_lm, g_rm, g_le, g_re, s_le, s_re, sums, news, send, recv = refs[4:]
    size, end = 2 * half, half + tile
    grid = Grid(send, recv)
    has = grid.has
    val = frame.at[:, half:end, half:end]
    up = grid.message("up", acc.at[:, :half, :], fb)
    down = grid.message("down", acc.at[:, end:, :], fa)
    mid = (tile - size) // 2
    mids = []
    for rank in range(2):
        at, to = slice(size + rank * mid, size + (rank + 1) * mid), slice(rank * mid, (rank + 1) * mid)
        mids.append(grid.strip("left", rank, acc.at[:, at, :half], g_rm.at[:, to], sums.at[rank, :, :mid]))
        mids.append(grid.strip("right", rank, acc.at[:, at, end:], g_lm.at[:, to], sums.at[rank, :, :mid]))
    ends = []
    for at in range(2):
        via = sums.at[2] if at == 0 else None
        ends.append(grid.strip("left", 2 + at, s_le.at[:, at], g_re.at[:, at], via))
        ends.append(grid.strip("right", 2 + at, s_re.at[:, at], g_le.at[:, at], via))
    via = [news.at[0, :, :mid], news.at[1, :, :mid], news.at[2]]
    new_ends, new_inner = column_messages(grid, tile, half, val, frame, via)
    new_rows = row_messages(grid, tile, half, val, frame)
    corners = corner_messages(grid, tile, half, frame)
    grid.greet()
    each("begin", *mids)
    start(up, down)
    each("rest", *mids)
    clear_beyond(grid, tile, half, frame)
    for side, buffers in (("up", (fa,)), ("down", (fb,)), ("left", (g_lm, g_le)), ("right", (g_rm, g_re))):

        @pl.when(jnp.logical_not(has[side]))
        def _():
            for b in buffers:
                b[...] = jnp.zeros_like(b)

    arrive(up, down)
    for ch in range(2):
        s_le[ch, 0] = acc[ch, half:size, :half] + fa[ch, :, :half]
        s_le[ch, 1] = acc[ch, tile:end, :half] + fb[ch, :, :half]
        s_re[ch, 0] = acc[ch, half:size, end:] + fa[ch, :, end:]
        s_re[ch, 1] = acc[ch, tile:end, end:] + fb[ch, :, end:]
    start(*ends)
    tops, bottoms, inner = slice(0, half), slice(tile - half, tile), slice(half, tile - half)
    heads, tails = slice(0, half), slice(tile - half, tile)

    def moved(at):
        return slice(at.start + half, at.stop + half)

    def settle(ch, rows, cols, more):
        total = acc[ch, moved(rows), moved(cols)] + BETA * cells[ch, rows, cols]
        for m in more:
            total = total + m
        frame[ch, moved(rows), moved(cols)] = total / weight[rows, cols]

    forward(*mids)
    for ch in range(2):
        settle(ch, inner, inner, ())
        settle(ch, tops, inner, (fa[ch, :, size:tile],))
        settle(ch, bottoms, inner, (fb[ch, :, size:tile],))
    arrive(*mids)
    for ch in range(2):
        settle(ch, inner, heads, (g_lm[ch],))
        settle(ch, inner, tails, (g_rm[ch],))
    first, second = [], new_inner
    forward(*ends)
    arrive(*ends)
    for ch in range(2):
        settle(ch, tops, heads, (fa[ch, :, half:size], g_le[ch, 0]))
        settle(ch, bottoms, heads, (fb[ch, :, half:size], g_le[ch, 1]))
        settle(ch, tops, tails, (fa[ch, :, tile:end], g_re[ch, 0]))
        settle(ch, bottoms, tails, (fb[ch, :, tile:end], g_re[ch, 1]))
    each("begin", *new_ends, *second)
    each("rest", *new_ends)
    start(*new_rows)
    forward(*first)
    each("begun", *new_ends, *second)
    each("rest", *second)
    forward(*new_ends, *second)
    arrive(*new_ends)
    start(*corners)
    arrive(*new_inner, *new_rows, *corners)
    each("begun", *mids, *ends, *first)
    leave(up, down, *mids, *ends, *new_ends, *new_inner, *new_rows, *corners)


def project_kernel(tile, half, offsets, count, *refs):
    dual, ext, probe, amp, wt = refs[:5]
    base, acc = refs[6:]
    slots = dual.shape[1]
    size = 2 * half
    live = count[0, 0]

    def skip(slot, carry):
        base[:, slot] = dual[:, slot]
        return carry

    def many(slots_at):
        tops = [offsets[0, 0, 0, at] for at in slots_at]
        lefts = [offsets[1, 0, 0, at] for at in slots_at]
        fwd, inv, fwd_odd, inv_odd = ((wt[2 * at], wt[2 * at + 1]) for at in range(4))
        n = range(len(slots_at))
        x = []
        for at, top, left in zip(slots_at, tops, lefts):
            pr, pi = probe[0], probe[1]
            wr = load_window(ext, 0, top, left, size)
            wi = load_window(ext, 1, top, left, size)
            re = pr * wr - pi * wi + dual[0, at]
            im = pr * wi + pi * wr + dual[1, at]
            x.append(cat([re[:half] + re[half:], im[:half] + im[half:]], 0))
            x.append(cat([re[:half] - re[half:], im[:half] - im[half:]], 0))
        y = [left_dot(*(fwd_odd if at % 2 else fwd), v) for at, v in enumerate(x)]
        x = []
        for i in n:
            even, odd = y[2 * i], y[2 * i + 1]
            re = cat([even[:half], odd[:half]], 0)
            im = cat([even[half:], odd[half:]], 0)
            x.append(cat([re[:, :half] + re[:, half:], im[:, :half] + im[:, half:]], 1))
            x.append(cat([re[:, :half] - re[:, half:], im[:, :half] - im[:, half:]], 1))
        y = [right_dot(v, *(inv_odd if at % 2 else inv)) for at, v in enumerate(x)]
        x = []
        for i, at in enumerate(slots_at):
            for odd in range(2):
                b = amp[at, odd * size : (odd + 1) * size]
                v = y[2 * i + odd]
                re, im = v[:, :half], v[:, half:]
                fac = b * lax.rsqrt(jnp.maximum(re * re + im * im, FLOOR * FLOOR))
                x.append(cat([re * fac, im * fac], 1))
        y = [right_dot(v, *(fwd_odd if at % 2 else fwd)) for at, v in enumerate(x)]
        x = []
        for i in n:
            even, odd = y[2 * i], y[2 * i + 1]
            re = cat([even[:, :half] + odd[:, :half], even[:, :half] - odd[:, :half]], 1)
            im = cat([even[:, half:] + odd[:, half:], even[:, half:] - odd[:, half:]], 1)
            x.append(cat([re[:half], im[:half]], 0))
            x.append(cat([re[half:], im[half:]], 0))
        y = [left_dot(*(inv_odd if at % 2 else inv), v) for at, v in enumerate(x)]
        for i, (at, top, left) in enumerate(zip(slots_at, tops, lefts)):
            even, odd = y[2 * i], y[2 * i + 1]
            dr = cat([even[:half] + odd[:half], even[:half] - odd[:half]], 0) - dual[0, at]
            di = cat([even[half:] + odd[half:], even[half:] - odd[half:]], 0) - dual[1, at]
            base[0, at] = -dr
            base[1, at] = -di
            pr, pi = probe[0], probe[1]
            add_window(acc, 0, top, left, pr * dr + pi * di)
            add_window(acc, 1, top, left, pr * di - pi * dr)

    whole = 4 * (live // 4)

    def four(index, carry):
        many([4 * index + at for at in range(4)])
        return carry

    lax.fori_loop(live, slots, skip, 0)
    lax.fori_loop(0, live // 4, four, 0)

    @pl.when(live - whole >= 2)
    def _():
        many([whole, whole + 1])

    @pl.when(live % 2 == 1)
    def _():
        many([live - 1])


def dual_kernel(tile, half, offsets, live, ext, probe, base, out, new, ready, sems):
    slots = base.shape[1]
    size = 2 * half
    keep = pltpu.make_async_copy(ext.at[:, half : half + tile, half : half + tile], new, sems.at[slots])
    keep.start()
    copies = []
    for slot in range(slots):
        copy = pltpu.make_async_copy(ready.at[slot], out.at[:, slot], sems.at[slot])
        copies.append(copy)
        active = slot < live[0, 0]

        @pl.when(jnp.logical_not(active))
        def _():
            ready[slot] = base[:, slot]

        @pl.when(active)
        def _():
            top = offsets[0, 0, 0, slot]
            left = offsets[1, 0, 0, slot]
            pr, pi = probe[0], probe[1]
            sr = load_window(ext, 0, top, left, size)
            si = load_window(ext, 1, top, left, size)
            ready[slot, 0] = base[0, slot] + (pr * sr - pi * si)
            ready[slot, 1] = base[1, slot] + (pr * si + pi * sr)

        copy.start()
    for copy in copies:
        copy.wait()
    keep.wait()


def shards(object_field, probe, dual, amplitude, offsets, live):
    tile = object_field.shape[1]
    size = probe.shape[1]
    half = size // 2
    slots = dual.shape[3]
    wide = tile + size
    mid = tile - size
    amps = amplitude.reshape(slots, size, size)
    sd = lambda *shape: jax.ShapeDtypeStruct(shape, F32)
    dma = lambda n: pltpu.SemaphoreType.DMA((n,))
    wt = tables(size)
    fixed = lambda x: pltpu.with_memory_space_constraint(x, pltpu.HBM)

    frame, lam, wt, probe, weight, acc, amps = pl.pallas_call(
        functools.partial(halo_kernel, tile, half),
        out_shape=(
            sd(2, wide, wide),
            sd(2, slots, size, size),
            jax.ShapeDtypeStruct(wt.shape, wt.dtype),
            sd(2, size, size),
            sd(tile, tile),
            sd(2, wide, wide),
            sd(slots, 2 * size, half),
        ),
        in_specs=[HBM, SM, HBM, HBM, HBM, HBM, HBM],
        out_specs=(VM,) * 7,
        scratch_shapes=[
            pltpu.SMEM(offsets.shape, jnp.int32),
            pltpu.VMEM((3, 3, ROWS, LANES), jnp.int32),
            pltpu.VMEM((ROWS, LANES), jnp.int32),
            pltpu.VMEM((slots, size, size), F32),
            pltpu.VMEM((size // LANES, size, LANES), F32),
            pltpu.VMEM((2, mid // 2, half), F32),
            pltpu.VMEM((2, mid // 2, half), F32),
            pltpu.VMEM((2, half, half), F32),
            dma(40),
            dma(40),
            dma(6),
        ],
        compiler_params=pltpu.CompilerParams(collective_id=0, has_side_effects=True, vmem_limit_bytes=16 * MIB),
        cost_estimate=pl.CostEstimate(flops=0, bytes_accessed=80_000_000, transcendentals=0),
        name="halo",
    )(fixed(offsets), live, fixed(object_field), fixed(dual.reshape(2, slots, size, size)), fixed(wt), fixed(probe), fixed(amps))

    cost = lambda size: pl.CostEstimate(flops=0, bytes_accessed=size, transcendentals=0)
    base, acc = pl.pallas_call(
        functools.partial(project_kernel, tile, half),
        out_shape=(sd(2, slots, size, size), sd(2, wide, wide)),
        in_specs=[SM, SM] + [VM] * 6,
        out_specs=(VM, VM),
        input_output_aliases={7: 1},
        compiler_params=pltpu.CompilerParams(vmem_limit_bytes=20 * MIB),
        cost_estimate=cost(30_000_000),
        name="project",
    )(offsets, live, lam, frame, probe, amps, wt, acc)

    strip, side, end, via = (2, half, wide), (2, mid, half), (2, 2, half, half), (3, 2, max(half, mid // 2), half)
    frame = pl.pallas_call(
        functools.partial(update_kernel, tile, half),
        out_shape=sd(2, wide, wide),
        in_specs=[VM] * 3,
        out_specs=VM,
        scratch_shapes=[pltpu.VMEM(x, F32) for x in (strip, strip, side, side, end, end, end, end, via, via)] + [dma(60), dma(60)],
        compiler_params=pltpu.CompilerParams(collective_id=1, has_side_effects=True, vmem_limit_bytes=8 * MIB),
        cost_estimate=cost(150_000_000),
        name="update",
    )(acc, object_field, weight)

    dual_new, new = pl.pallas_call(
        functools.partial(dual_kernel, tile, half),
        out_shape=(sd(2, slots, size, size), sd(2, tile, tile)),
        in_specs=[SM, SM, VM, VM, VM],
        out_specs=(ANY, ANY),
        scratch_shapes=[pltpu.VMEM((slots, 2, size, size), F32), dma(slots + 1)],
        compiler_params=pltpu.CompilerParams(vmem_limit_bytes=12 * MIB),
        name="renew",
    )(offsets, live, frame, probe, base)
    return new, dual_new.reshape(dual.shape)


def solution(mesh):
    placed = (
        P(None, "row", "col"),
        P(),
        P(None, "row", "col", None, None, None),
        P("row", "col", None, None, None),
        P(None, "row", "col", None),
        P("row", "col"),
    )
    return jax.shard_map(
        shards,
        mesh=mesh,
        in_specs=placed,
        out_specs=(P(None, "row", "col"), P(None, "row", "col", None, None, None)),
        check_vma=False,
    )
```

```python
import functools
import math

import jax
import jax.numpy as jnp
import numpy as np
from jax import lax
from jax.experimental import pallas as pl
from jax.experimental.pallas import tpu as pltpu
from jax.sharding import PartitionSpec as P

FLOOR = 0.1
BETA = 1.0
LANES = 128
ROWS = 8
MIB = 1 << 20
F32 = jnp.float32
BF16 = jnp.bfloat16
ANY = pl.BlockSpec(memory_space=pl.ANY)
VM = pl.BlockSpec(memory_space=pltpu.VMEM)
SM = pl.BlockSpec(memory_space=pltpu.SMEM)
HBM = pl.BlockSpec(memory_space=pltpu.HBM)


def tables(size):
    n = size // 2
    k = np.arange(n)
    angle = 2.0 * math.pi * ((k[:, None] * k[None, :]) % n) / n
    c, s = np.cos(angle) / math.sqrt(size), np.sin(angle) / math.sqrt(size)
    fwd = np.block([[c, s], [-s, c]])
    inv = np.block([[c, -s], [s, c]])
    angle = angle + 2.0 * math.pi * k[None, :] / size
    c, s = np.cos(angle) / math.sqrt(size), np.sin(angle) / math.sqrt(size)
    odd = np.block([[c, s], [-s, c]])
    parts = []
    for full in (fwd, inv, odd, odd.T):
        hi = full.astype(np.float32).astype(BF16)
        parts += [hi, (full - hi.astype(np.float64)).astype(np.float32).astype(BF16)]
    perm = np.zeros((size, size), np.float32)
    perm[2 * k, k] = 1.0
    perm[2 * k + 1, n + k] = 1.0
    return jnp.asarray(np.stack(parts + [perm.astype(BF16)]))


def split(x):
    hi = x.astype(BF16)
    return hi, (x - hi.astype(F32)).astype(BF16)


def dot(a, b):
    return jnp.dot(a, b, preferred_element_type=F32)


def left_dot(wh, wl, x):
    xh, xl = split(x)
    return dot(wl, xh) + dot(wh, xl) + dot(wh, xh)


def right_dot(x, wh, wl):
    xh, xl = split(x)
    return dot(xh, wl) + dot(xl, wh) + dot(xh, wh)


def cat(parts, axis):
    return jnp.concatenate(parts, axis=axis)


def load_window(ext, channel, top, left, size):
    row = pl.multiple_of((top // ROWS) * ROWS, ROWS)
    base = pl.multiple_of((left // LANES) * LANES, LANES)
    width, height = size + LANES, size + ROWS
    wide = ext[channel, pl.ds(row, height), pl.ds(base, width)]
    wide = pltpu.roll(wide, (width - (left - base)) % width, 1)[:, :size]
    return pltpu.roll(wide, (height - (top - row)) % height, 0)[:size]


def add_window(acc, channel, top, left, value):
    size = value.shape[0]
    row = pl.multiple_of((top // ROWS) * ROWS, ROWS)
    base = pl.multiple_of((left // LANES) * LANES, LANES)
    width, height = size + LANES, size + ROWS
    wide = cat([value, jnp.zeros((ROWS, size), F32)], 0)
    wide = pltpu.roll(wide, top - row, 0)
    wide = cat([wide, jnp.zeros((height, LANES), F32)], 1)
    wide = pltpu.roll(wide, left - base, 1)
    acc[channel, pl.ds(row, height), pl.ds(base, width)] += wide


def clear_beyond(grid, tile, half, frame):
    end = half + tile
    strips = (
        ("up", slice(0, half), slice(None)),
        ("down", slice(end, None), slice(None)),
        ("left", slice(half, end), slice(0, half)),
        ("right", slice(half, end), slice(end, None)),
    )
    for side, rows, cols in strips:

        @pl.when(jnp.logical_not(grid.has[side]))
        def _():
            frame[:, rows, cols] = jnp.zeros_like(frame[:, rows, cols])

    for up, rows in (("up", slice(0, half)), ("down", slice(end, None))):
        for side, cols in (("left", slice(0, half)), ("right", slice(end, None))):

            @pl.when(grid.has[up] & jnp.logical_not(grid.has[side]))
            def _():
                frame[:, rows, cols] = jnp.zeros_like(frame[:, rows, cols])


CHUNKS = 4


class Grid:
    def __init__(self, send, recv):
        row, col = lax.axis_index("row"), lax.axis_index("col")
        self.col, self.cols = col, lax.axis_size("col")
        self.has = {
            "up": row > 0,
            "down": row < lax.axis_size("row") - 1,
            "left": col > 0,
            "right": col < self.cols - 1,
        }
        self.peer = {"up": {"row": row - 1}, "down": {"row": row + 1}, "left": {"col": col - 1}, "right": {"col": col + 1}}
        self.back = {"up": "down", "down": "up", "left": "right", "right": "left"}
        self.step = {"left": -1, "right": 1}
        self.send, self.recv = send, recv
        self.count = 0

    def bends(self):
        return self.cols % 2 == 0 and self.cols > 2

    def relayed(self, col, side, rank):
        gaps = self.cols // 2 - 1
        if side == "right":
            share = CHUNKS * (gaps - col // 2) // (gaps + 1)
            return (col % 2 == 1) & (col > 0) & (col < self.cols - 1) & (rank < share)
        share = CHUNKS * (col // 2) // (gaps + 1)
        return (col % 2 == 0) & (col > 0) & (col < self.cols) & (rank < share)

    def greet(self, between=None):
        barrier = pltpu.get_barrier_semaphore()
        col = self.col
        signals = [(self.has[side], self.peer[side]) for side in self.has]
        waits = sum(h.astype(jnp.int32) for h in self.has.values())
        if self.bends():
            signals.append((self.relayed(col - 1, "right", 0), {"col": col - 2}))
            signals.append((self.relayed(col + 1, "left", 0), {"col": col + 2}))
            waits += self.relayed(col + 1, "right", 0).astype(jnp.int32)
            waits += self.relayed(col - 1, "left", 0).astype(jnp.int32)
        for goes, peer in signals:

            @pl.when(goes)
            def _():
                pl.semaphore_signal(barrier, inc=1, device_id=peer, device_id_type=pl.DeviceIdType.MESH)

        if between is not None:
            between()
        pl.semaphore_wait(barrier, waits)

    def copy(self, peer, src, dst):
        at = self.count
        self.count += 1
        return pltpu.make_async_remote_copy(
            src_ref=src,
            dst_ref=dst,
            send_sem=self.send.at[at],
            recv_sem=self.recv.at[at],
            device_id=peer,
            device_id_type=pl.DeviceIdType.MESH,
        )

    def message(self, side, src, dst, also=None):
        goes, comes = self.has[side], self.has[self.back[side]]
        if also is not None:
            goes, comes = goes & self.has[also], comes & self.has[also]
        return self.copy(self.peer[side], src, dst), goes, comes

    def strip(self, side, rank, src, dst, relay):
        return Strip(self, side, rank, src, dst, relay)


class Strip:
    def __init__(self, grid, side, rank, src, dst, relay):
        step, col = grid.step[side], grid.col
        goes, comes = grid.has[side], grid.has[grid.back[side]]
        self.hops = []
        if grid.bends() and relay is not None:
            first, then, last = (grid.relayed(col + step * at, side, rank) for at in (0, 1, -1))
            goes, comes = goes & jnp.logical_not(first), comes & jnp.logical_not(last)
            self.hops.append((grid.copy({"col": col - step}, src, relay), first, then))
            self.hops.append((grid.copy({"col": col + 2 * step}, relay, dst), then, last))
        self.direct = grid.copy(grid.peer[side], src, dst), goes, comes

    def begin(self):
        start(*self.hops[:1])

    def begun(self):
        leave(*self.hops[:1])

    def rest(self):
        start(self.direct)

    def start(self):
        self.begin()
        self.rest()

    def forward(self):
        if self.hops:
            (first, _, comes), (then, _, _) = self.hops

            @pl.when(comes)
            def _():
                first.wait_recv()
                then.start()

    def arrive(self):
        arrive(*self.hops[1:], self.direct)

    def leave(self):
        leave(*self.hops[1:], self.direct)


def when(cond, act):
    if cond is True:
        act()
    else:
        pl.when(cond)(act)


def start(*messages):
    for m in messages:
        if isinstance(m, Strip):
            m.start()
        else:
            pl.when(m[1])(m[0].start)


def each(act, *strips):
    for m in strips:
        getattr(m, act)()


def forward(*strips):
    each("forward", *strips)


def arrive(*messages):
    for m in messages:
        if isinstance(m, Strip):
            m.arrive()
        else:
            pl.when(m[2])(m[0].wait_recv)


def leave(*messages):
    for m in messages:
        if isinstance(m, Strip):
            m.leave()
        else:
            pl.when(m[1])(m[0].wait_send)


def column_messages(grid, tile, half, src, frame, relay):
    size, end = 2 * half, half + tile
    mid = (tile - size) // 2
    rows = [slice(half, half + mid), slice(half + mid, tile - half), slice(0, half), slice(tile - half, tile)]
    groups = []
    for rank, at in enumerate(rows):
        store = slice(at.start + half, at.stop + half)
        via = relay[rank] if rank < len(relay) else None
        groups.append(
            [
                grid.strip("left", rank, src.at[:, at, :half], frame.at[:, store, end:], via),
                grid.strip("right", rank, src.at[:, at, tile - half :], frame.at[:, store, :half], via),
            ]
        )
    return groups[2] + groups[3], groups[0] + groups[1]


def row_messages(grid, tile, half, src, frame):
    end = half + tile
    return [
        grid.message("up", src.at[:, :half, :], frame.at[:, end:, half:end]),
        grid.message("down", src.at[:, tile - half :, :], frame.at[:, :half, half:end]),
    ]


def corner_messages(grid, tile, half, frame):
    size, end = 2 * half, half + tile
    out = []
    for side, cols in (("left", slice(0, half)), ("right", slice(end, None))):
        out.append(grid.message("up", frame.at[:, half:size, cols], frame.at[:, end:, cols], also=side))
        out.append(grid.message("down", frame.at[:, tile:end, cols], frame.at[:, :half, cols], also=side))
    return out


def one_hot(shape, shift):
    gap = lax.broadcasted_iota(jnp.int32, shape, 0) - lax.broadcasted_iota(jnp.int32, shape, 1)
    return jnp.where(gap == shift, 1.0, 0.0).astype(BF16)


def spread_power(tile, half, slots, bands, infos, probe, weight):
    size = 2 * half
    high, low = split(probe[0] * probe[0] + probe[1] * probe[1])
    spans = [
        (slice(0, half), slice(half, size), -tile),
        (slice(0, tile), slice(0, size), 0),
        (slice(tile - half, tile), slice(0, half), tile),
    ]
    for r in bands:
        rows, along, row_at = spans[r]
        for c, (cols, across, col_at) in enumerate(spans):
            ny, nk = rows.stop - rows.start, along.stop - along.start
            nx, nl = cols.stop - cols.start, across.stop - across.start
            part = cat([high[along, across], low[along, across]], 0)
            total = weight[rows, cols]
            for slot in range(slots):
                used = slot < infos[r, c, :1, 2 * slots : 2 * slots + 1]
                top = infos[r, c, :1, slot : slot + 1] + (row_at - half - rows.start + along.start)
                left = infos[r, c, :1, slots + slot : slots + slot + 1] + (col_at - half - cols.start + across.start)
                top = jnp.where(used, top, 2 * tile)
                moved = dot(part, one_hot((nl, nx), -left)).astype(BF16)
                place = one_hot((ny, nk), top)
                total = total + dot(place, moved[:nk]) + dot(place, moved[nk:])
            weight[rows, cols] = total


def sort_amplitude(slots, amp, strips, perm, out):
    count, size = strips.shape[0], strips.shape[1]
    half = size // 2
    for slot in range(slots):
        for c in range(count):
            strips[c] = amp[slot, :, c * LANES : (c + 1) * LANES]
        rows = []
        for first in range(2):
            rows.append(cat([strips[c, pl.ds(first, half, stride=2), :] for c in range(count)], 1))
        high, low = split(cat(rows, 0))
        a = dot(high, perm) + dot(low, perm)
        out[slot] = cat([a[:, :half], a[:, half:]], 0)


def halo_kernel(tile, half, places, live, cells, dual, wt, probe, amp, *refs):
    frame, lam, tables_out, probe_out, weight, acc, sorted_amp = refs[:7]
    offsets, infos, tag, plain_amp, strips, r0, r1, r2, send, recv, local = refs[7:]
    grid = Grid(send, recv)
    has = grid.has
    slots = offsets.shape[3]
    scalars = pltpu.make_async_copy(places, offsets, local.at[5])
    scalars.start()
    loads = [
        pltpu.make_async_copy(probe, probe_out, local.at[0]),
        pltpu.make_async_copy(cells, frame.at[:, half : half + tile, half : half + tile], local.at[1]),
        pltpu.make_async_copy(dual, lam, local.at[2]),
        pltpu.make_async_copy(wt, tables_out, local.at[3]),
        pltpu.make_async_copy(amp, plain_amp, local.at[4]),
    ]
    ends, inner = column_messages(grid, tile, half, cells, frame, (r0, r1, r2))
    rows = row_messages(grid, tile, half, cells, frame)
    corners = corner_messages(grid, tile, half, frame)
    tags = [
        grid.message("left", tag, infos.at[1, 2]),
        grid.message("right", tag, infos.at[1, 0]),
    ]
    bands = [
        grid.message("up", infos.at[1], infos.at[2]),
        grid.message("down", infos.at[1], infos.at[0]),
    ]

    def make_tag():
        scalars.wait()
        lane = lax.broadcasted_iota(jnp.int32, tag.shape, 1)
        value = jnp.where(lane == 2 * slots, live[0, 0], 0)
        for k in range(slots):
            value = jnp.where(lane == k, offsets[0, 0, 0, k], value)
            value = jnp.where(lane == slots + k, offsets[1, 0, 0, k], value)
        tag[...] = value
        infos[1, 1] = value

    grid.greet(make_tag)
    start(*tags)
    each("begin", *inner, *ends)
    each("rest", *ends)
    for copy in loads:
        copy.start()
    clear_beyond(grid, tile, half, frame)
    for side, at in (("left", (1, 0)), ("right", (1, 2)), ("up", (0,)), ("down", (2,))):

        @pl.when(jnp.logical_not(has[side]))
        def _():
            infos[at] = jnp.zeros_like(infos[at])

    arrive(*tags)
    start(*bands, *rows)
    each("begun", *inner, *ends)
    each("rest", *inner)
    forward(*inner, *ends)
    loads[0].wait()
    arrive(*bands)
    acc[...] = jnp.zeros_like(acc)
    weight[...] = jnp.full_like(weight, BETA)
    spread_power(tile, half, slots, (0, 2), infos, probe_out, weight)
    arrive(*ends)
    start(*corners)
    spread_power(tile, half, slots, (1,), infos, probe_out, weight)
    for copy in loads[1:]:
        copy.wait()
    sort_amplitude(slots, plain_amp, strips, tables_out[8], sorted_amp)
    arrive(*inner, *rows, *corners)
    leave(*tags, *ends, *inner, *rows, *bands, *corners)


def update_kernel(tile, half, *refs):
    acc, cells, weight, frame = refs[:4]
    fa, fb, g_lm, g_rm, g_le, g_re, s_le, s_re, sums, news, send, recv = refs[4:]
    size, end = 2 * half, half + tile
    grid = Grid(send, recv)
    has = grid.has
    val = frame.at[:, half:end, half:end]
    edges, rest = [], []
    for cols, group in ((slice(0, half), edges), (slice(end, end + half), edges), (slice(half, end), rest)):
        group.append(grid.message("up", acc.at[:, :half, cols], fb.at[:, :, cols]))
        group.append(grid.message("down", acc.at[:, end:, cols], fa.at[:, :, cols]))
    mid = (tile - size) // 2
    mids = []
    for rank in range(2):
        at, to = slice(size + rank * mid, size + (rank + 1) * mid), slice(rank * mid, (rank + 1) * mid)
        mids.append(grid.strip("left", rank, acc.at[:, at, :half], g_rm.at[:, to], sums.at[rank, :, :mid]))
        mids.append(grid.strip("right", rank, acc.at[:, at, end:], g_lm.at[:, to], sums.at[rank, :, :mid]))
    ends = []
    for at in range(2):
        via = sums.at[2] if at == 0 else None
        ends.append(grid.strip("left", 2 + at, s_le.at[:, at], g_re.at[:, at], via))
        ends.append(grid.strip("right", 2 + at, s_re.at[:, at], g_le.at[:, at], via))
    via = [news.at[0, :, :mid], news.at[1, :, :mid], news.at[2]]
    new_ends, new_inner = column_messages(grid, tile, half, val, frame, via)
    new_rows = row_messages(grid, tile, half, val, frame)
    corners = corner_messages(grid, tile, half, frame)
    grid.greet()
    each("begin", *mids)
    start(*edges, *rest)
    each("rest", *mids)
    clear_beyond(grid, tile, half, frame)
    for side, buffers in (("up", (fa,)), ("down", (fb,)), ("left", (g_lm, g_le)), ("right", (g_rm, g_re))):

        @pl.when(jnp.logical_not(has[side]))
        def _():
            for b in buffers:
                b[...] = jnp.zeros_like(b)

    forward(*mids)
    arrive(*edges)
    for ch in range(2):
        s_le[ch, 0] = acc[ch, half:size, :half] + fa[ch, :, :half]
        s_le[ch, 1] = acc[ch, tile:end, :half] + fb[ch, :, :half]
        s_re[ch, 0] = acc[ch, half:size, end:] + fa[ch, :, end:]
        s_re[ch, 1] = acc[ch, tile:end, end:] + fb[ch, :, end:]
    start(*ends)
    tops, bottoms, inner = slice(0, half), slice(tile - half, tile), slice(half, tile - half)
    heads, tails = slice(0, half), slice(tile - half, tile)

    def moved(at):
        return slice(at.start + half, at.stop + half)

    def settle(ch, rows, cols, more):
        total = acc[ch, moved(rows), moved(cols)] + BETA * cells[ch, rows, cols]
        for m in more:
            total = total + m
        frame[ch, moved(rows), moved(cols)] = total / weight[rows, cols]

    for ch in range(2):
        settle(ch, inner, inner, ())
    arrive(*rest)
    for ch in range(2):
        settle(ch, tops, inner, (fa[ch, :, size:tile],))
        settle(ch, bottoms, inner, (fb[ch, :, size:tile],))
    arrive(*mids)
    for ch in range(2):
        settle(ch, inner, heads, (g_lm[ch],))
        settle(ch, inner, tails, (g_rm[ch],))
    first, second = [], new_inner
    forward(*ends)
    arrive(*ends)
    for ch in range(2):
        settle(ch, tops, heads, (fa[ch, :, half:size], g_le[ch, 0]))
        settle(ch, bottoms, heads, (fb[ch, :, half:size], g_le[ch, 1]))
        settle(ch, tops, tails, (fa[ch, :, tile:end], g_re[ch, 0]))
        settle(ch, bottoms, tails, (fb[ch, :, tile:end], g_re[ch, 1]))
    each("begin", *new_ends, *second)
    each("rest", *new_ends)
    start(*new_rows)
    forward(*first)
    each("begun", *new_ends, *second)
    each("rest", *second)
    forward(*new_ends, *second)
    arrive(*new_ends)
    start(*corners)
    arrive(*new_inner, *new_rows, *corners)
    each("begun", *mids, *ends, *first)
    leave(*edges, *rest, *mids, *ends, *new_ends, *new_inner, *new_rows, *corners)


def project_kernel(tile, half, offsets, count, *refs):
    dual, ext, probe, amp, wt = refs[:5]
    base, acc = refs[6:]
    slots = dual.shape[1]
    size = 2 * half
    live = count[0, 0]

    def skip(slot, carry):
        base[:, slot] = dual[:, slot]
        return carry

    def many(slots_at):
        tops = [offsets[0, 0, 0, at] for at in slots_at]
        lefts = [offsets[1, 0, 0, at] for at in slots_at]
        fwd, inv, fwd_odd, inv_odd = ((wt[2 * at], wt[2 * at + 1]) for at in range(4))
        n = range(len(slots_at))
        x = []
        for at, top, left in zip(slots_at, tops, lefts):
            pr, pi = probe[0], probe[1]
            wr = load_window(ext, 0, top, left, size)
            wi = load_window(ext, 1, top, left, size)
            re = pr * wr - pi * wi + dual[0, at]
            im = pr * wi + pi * wr + dual[1, at]
            x.append(cat([re[:half] + re[half:], im[:half] + im[half:]], 0))
            x.append(cat([re[:half] - re[half:], im[:half] - im[half:]], 0))
        y = [left_dot(*(fwd_odd if at % 2 else fwd), v) for at, v in enumerate(x)]
        x = []
        for i in n:
            even, odd = y[2 * i], y[2 * i + 1]
            re = cat([even[:half], odd[:half]], 0)
            im = cat([even[half:], odd[half:]], 0)
            x.append(cat([re[:, :half] + re[:, half:], im[:, :half] + im[:, half:]], 1))
            x.append(cat([re[:, :half] - re[:, half:], im[:, :half] - im[:, half:]], 1))
        y = [right_dot(v, *(inv_odd if at % 2 else inv)) for at, v in enumerate(x)]
        x = []
        for i, at in enumerate(slots_at):
            for odd in range(2):
                b = amp[at, odd * size : (odd + 1) * size]
                v = y[2 * i + odd]
                re, im = v[:, :half], v[:, half:]
                fac = b * lax.rsqrt(jnp.maximum(re * re + im * im, FLOOR * FLOOR))
                x.append(cat([re * fac, im * fac], 1))
        y = [right_dot(v, *(fwd_odd if at % 2 else fwd)) for at, v in enumerate(x)]
        x = []
        for i in n:
            even, odd = y[2 * i], y[2 * i + 1]
            re = cat([even[:, :half] + odd[:, :half], even[:, :half] - odd[:, :half]], 1)
            im = cat([even[:, half:] + odd[:, half:], even[:, half:] - odd[:, half:]], 1)
            x.append(cat([re[:half], im[:half]], 0))
            x.append(cat([re[half:], im[half:]], 0))
        y = [left_dot(*(inv_odd if at % 2 else inv), v) for at, v in enumerate(x)]
        for i, (at, top, left) in enumerate(zip(slots_at, tops, lefts)):
            even, odd = y[2 * i], y[2 * i + 1]
            dr = cat([even[:half] + odd[:half], even[:half] - odd[:half]], 0) - dual[0, at]
            di = cat([even[half:] + odd[half:], even[half:] - odd[half:]], 0) - dual[1, at]
            base[0, at] = -dr
            base[1, at] = -di
            pr, pi = probe[0], probe[1]
            add_window(acc, 0, top, left, pr * dr + pi * di)
            add_window(acc, 1, top, left, pr * di - pi * dr)

    whole = 4 * (live // 4)

    def four(index, carry):
        many([4 * index + at for at in range(4)])
        return carry

    lax.fori_loop(live, slots, skip, 0)
    lax.fori_loop(0, live // 4, four, 0)

    @pl.when(live - whole >= 2)
    def _():
        many([whole, whole + 1])

    @pl.when(live % 2 == 1)
    def _():
        many([live - 1])


def dual_kernel(tile, half, offsets, live, ext, probe, base, out, new, ready, sems):
    slots = base.shape[1]
    size = 2 * half
    keep = pltpu.make_async_copy(ext.at[:, half : half + tile, half : half + tile], new, sems.at[slots])
    keep.start()
    copies = []
    for slot in range(slots):
        copy = pltpu.make_async_copy(ready.at[slot], out.at[:, slot], sems.at[slot])
        copies.append(copy)
        active = slot < live[0, 0]

        @pl.when(jnp.logical_not(active))
        def _():
            ready[slot] = base[:, slot]

        @pl.when(active)
        def _():
            top = offsets[0, 0, 0, slot]
            left = offsets[1, 0, 0, slot]
            pr, pi = probe[0], probe[1]
            sr = load_window(ext, 0, top, left, size)
            si = load_window(ext, 1, top, left, size)
            ready[slot, 0] = base[0, slot] + (pr * sr - pi * si)
            ready[slot, 1] = base[1, slot] + (pr * si + pi * sr)

        copy.start()
    for copy in copies:
        copy.wait()
    keep.wait()


def shards(object_field, probe, dual, amplitude, offsets, live):
    tile = object_field.shape[1]
    size = probe.shape[1]
    half = size // 2
    slots = dual.shape[3]
    wide = tile + size
    mid = tile - size
    amps = amplitude.reshape(slots, size, size)
    sd = lambda *shape: jax.ShapeDtypeStruct(shape, F32)
    dma = lambda n: pltpu.SemaphoreType.DMA((n,))
    wt = tables(size)
    fixed = lambda x: pltpu.with_memory_space_constraint(x, pltpu.HBM)

    frame, lam, wt, probe, weight, acc, amps = pl.pallas_call(
        functools.partial(halo_kernel, tile, half),
        out_shape=(
            sd(2, wide, wide),
            sd(2, slots, size, size),
            jax.ShapeDtypeStruct(wt.shape, wt.dtype),
            sd(2, size, size),
            sd(tile, tile),
            sd(2, wide, wide),
            sd(slots, 2 * size, half),
        ),
        in_specs=[HBM, SM, HBM, HBM, HBM, HBM, HBM],
        out_specs=(VM,) * 7,
        scratch_shapes=[
            pltpu.SMEM(offsets.shape, jnp.int32),
            pltpu.VMEM((3, 3, ROWS, LANES), jnp.int32),
            pltpu.VMEM((ROWS, LANES), jnp.int32),
            pltpu.VMEM((slots, size, size), F32),
            pltpu.VMEM((size // LANES, size, LANES), F32),
            pltpu.VMEM((2, mid // 2, half), F32),
            pltpu.VMEM((2, mid // 2, half), F32),
            pltpu.VMEM((2, half, half), F32),
            dma(40),
            dma(40),
            dma(6),
        ],
        compiler_params=pltpu.CompilerParams(collective_id=0, has_side_effects=True, vmem_limit_bytes=16 * MIB),
        cost_estimate=pl.CostEstimate(flops=0, bytes_accessed=80_000_000, transcendentals=0),
        name="halo",
    )(fixed(offsets), live, fixed(object_field), fixed(dual.reshape(2, slots, size, size)), fixed(wt), fixed(probe), fixed(amps))

    cost = lambda size: pl.CostEstimate(flops=0, bytes_accessed=size, transcendentals=0)
    base, acc = pl.pallas_call(
        functools.partial(project_kernel, tile, half),
        out_shape=(sd(2, slots, size, size), sd(2, wide, wide)),
        in_specs=[SM, SM] + [VM] * 6,
        out_specs=(VM, VM),
        input_output_aliases={7: 1},
        compiler_params=pltpu.CompilerParams(vmem_limit_bytes=20 * MIB),
        cost_estimate=cost(30_000_000),
        name="project",
    )(offsets, live, lam, frame, probe, amps, wt, acc)

    strip, side, end, via = (2, half, wide), (2, mid, half), (2, 2, half, half), (3, 2, max(half, mid // 2), half)
    frame = pl.pallas_call(
        functools.partial(update_kernel, tile, half),
        out_shape=sd(2, wide, wide),
        in_specs=[VM] * 3,
        out_specs=VM,
        scratch_shapes=[pltpu.VMEM(x, F32) for x in (strip, strip, side, side, end, end, end, end, via, via)] + [dma(60), dma(60)],
        compiler_params=pltpu.CompilerParams(collective_id=1, has_side_effects=True, vmem_limit_bytes=8 * MIB),
        cost_estimate=cost(150_000_000),
        name="update",
    )(acc, object_field, weight)

    dual_new, new = pl.pallas_call(
        functools.partial(dual_kernel, tile, half),
        out_shape=(sd(2, slots, size, size), sd(2, tile, tile)),
        in_specs=[SM, SM, VM, VM, VM],
        out_specs=(ANY, ANY),
        scratch_shapes=[pltpu.VMEM((slots, 2, size, size), F32), dma(slots + 1)],
        compiler_params=pltpu.CompilerParams(vmem_limit_bytes=12 * MIB),
        name="renew",
    )(offsets, live, frame, probe, base)
    return new, dual_new.reshape(dual.shape)


def solution(mesh):
    placed = (
        P(None, "row", "col"),
        P(),
        P(None, "row", "col", None, None, None),
        P("row", "col", None, None, None),
        P(None, "row", "col", None),
        P("row", "col"),
    )
    return jax.shard_map(
        shards,
        mesh=mesh,
        in_specs=placed,
        out_specs=(P(None, "row", "col"), P(None, "row", "col", None, None, None)),
        check_vma=False,
    )
```
